32 devices in a mesh: groups: 2 (over y), blk: 4 (over z), subj: 4 (over x, core).
Axes of the slice: x: 2, y: 2, z: 4, core: 2. Of those that a mesh axis runs over, the one named last changes fastest.
Arguments:
- template_verts: float32 [3, 2048], P(None, ('groups', 'blk')), parts along dimension 1, may hold values from -6 to 6
- template_tris: int32 [3, 2048], P(None, ('groups', 'blk')), parts along dimension 1, may hold values from 0 to 255
- local_pairs: int32 [8, 2], P('blk'), may hold values 0 or 1
- partner_blocks: int32 [4, 8], P(None, 'blk'), may hold values from 0 to 1, as said below
- controls: float32 [3, 8192], replicated, may hold values from -6 to 6
- momenta: float32 [128, 3, 8192], P(('groups', 'subj')), parts along dimension 0, may hold values from -0.06 to 0.06
- target_verts: float32 [128, 3, 1024], P(('groups', 'subj'), None, 'blk'), parts along dimension 0, may hold values from -6 to 6
- target_tris: int32 [128, 3, 1024], P(('groups', 'subj'), None, 'blk'), parts along dimension 0, may hold values from 0 to 255
Outputs:
- template_grad: float32 [3, 2048], P(None, ('groups', 'blk')), parts along dimension 1
- momenta_grad: float32 [128, 3, 8192], P(('groups', 'subj'), None, 'blk'), parts along dimension 0
The draws below stay inside these ranges and needn't reach their ends.
There are 2 independent parts, one for each index of `groups`. The reference program is written for one: setup_inputs(seed, part) draws one part's arguments, and reference() takes and returns one part's arrays. A program takes and returns all parts, laid end to end along the dimension named above; an argument that names none is the same for every part. Nothing has to cross between parts.
Inputs may be any that keep to these rules, and one draw needn't show every extreme that they name: Corner k of template triangle t is template vertex (t // 256) * 256 + template_tris[k, t]; corners of one triangle may coincide. Corner k of triangle t of subject s is its vertex (t // 256) * 256 + target_tris[s, k, t]; corners may coincide. `partner_blocks`: for each r, shard d and its mate shard d XOR 2^(r mod L), the entries of the 2 blocks of d form a permutation of 0 to 1, and those of the mate shard its inverse, so that the pairing of blocks is mutual.
All inputs are finite; a program needn't handle non-finite values. No bound on the sum of `local_pairs` on one device may be relied on, other than what follows from the above.
Results may differ from the reference program's by a relative error of at most 0.0001.
Values sent between devices are 32-bit elements; how exact they have to be, the bound alone decides.
A program may use at most 64 MiB of HBM per device.

```python
import jax
import jax.numpy as jnp
from jax import lax

BLK = 128
BLK_DEV = 2
CTRL = 8192
SHARDS = 4
ELEMS = 256
BLOCKS = 8
VERTS = 1024
SUBJ = 64


def draw_partner_blocks(key, part):
    shards = BLOCKS // BLK_DEV
    bit_count = max(shards.bit_length() - 1, 1)
    rounds = []
    for r in range(4):
        round_key = jax.random.fold_in(key, 100 + r)
        scores = jax.random.randint(round_key, (shards, BLK_DEV), 0, 1 << 20)
        scores = scores * BLK_DEV + jnp.arange(BLK_DEV, dtype=jnp.int32)[None]
        forward = jnp.argsort(scores, axis=1).astype(jnp.int32)
        shard_ids = jnp.arange(shards, dtype=jnp.int32)
        mate_ids = shard_ids ^ 1 << r % bit_count
        lower_ids = jnp.minimum(shard_ids, mate_ids)
        chosen = forward[lower_ids]
        inverse = jnp.argsort(chosen, axis=1).astype(jnp.int32)
        result = jnp.where((shard_ids <= mate_ids)[:, None], chosen, inverse)
        rounds.append(result.reshape(-1))
    return jnp.stack(rounds).astype(jnp.int32)


def set_ends(drawn, own_key, smallest, largest):
    index_at = [jax.random.randint(jax.random.fold_in(own_key, axis), (), 0, length) for axis, length in enumerate(drawn.shape)]
    widest = drawn.shape.index(max(drawn.shape))
    beside = index_at[:widest] + [(index_at[widest] + 1) % drawn.shape[widest]] + index_at[widest + 1:]
    return drawn.at[tuple(index_at)].set(smallest).at[tuple(beside)].set(largest)


def shard_levels(rng, dims, pieces, smallest, largest):
    def one(position, parts):
        heights = jax.random.uniform(jax.random.fold_in(jax.random.fold_in(rng, 6), position), (parts,), jnp.float32, smallest / len(pieces), largest / len(pieces))
        return jnp.repeat(jnp.exp(heights), dims[position] // parts).reshape((-1,) + (1,) * (len(dims) - position - 1))

    factor_of = one(*pieces[0])
    for cut in pieces[1:]:
        factor_of = factor_of * one(*cut)
    return factor_of


def gaussian(rng, dims, scale, bound, cuts=(), held_as=jnp.bfloat16):
    values = scale * jax.random.normal(rng, dims, jnp.float32)
    if cuts:
        values = values * shard_levels(rng, dims, cuts, -0.22, 0.18)
    return jnp.clip(values, -bound, bound).astype(held_as)


def setup_inputs(seed: int = 0, part: int = 0) -> dict:
    streams_of = jax.random.split(jax.random.key(seed), 9)
    part_keys = jax.random.split(jax.random.fold_in(streams_of[8], part), 9)
    template_verts = gaussian(part_keys[0], (3, VERTS), 1.0, 6.0, ((1, 4),), jnp.float32)
    template_tris = set_ends(jax.random.randint(part_keys[1], (3, VERTS), 0, ELEMS), jax.random.fold_in(part_keys[1], 1), 0, ELEMS - 1).astype(jnp.int32)
    local_pairs = set_ends((jax.random.randint(streams_of[2], (BLOCKS, BLK_DEV), 0, 2) < 1).astype(jnp.int32), jax.random.fold_in(streams_of[2], 1), 0, 1)
    partner_blocks = draw_partner_blocks(jax.random.fold_in(streams_of[8], 71), part)
    controls = gaussian(streams_of[4], (3, CTRL), 1.0, 6.0, (), jnp.float32)
    momenta = gaussian(part_keys[5], (SUBJ, 3, CTRL), 0.01, 0.06, ((0, 4),), jnp.float32)
    target_verts = gaussian(part_keys[6], (SUBJ, 3, VERTS), 1.0, 6.0, ((0, 4), (2, 4)), jnp.float32)
    target_tris = set_ends(jax.random.randint(part_keys[7], (SUBJ, 3, VERTS), 0, ELEMS), jax.random.fold_in(part_keys[7], 1), 0, ELEMS - 1).astype(jnp.int32)
    return {"template_verts": template_verts, "template_tris": template_tris, "local_pairs": local_pairs, "partner_blocks": partner_blocks, "controls": controls, "momenta": momenta, "target_verts": target_verts, "target_tris": target_tris}


precise = lax.Precision.HIGHEST
AREA_SQ = 0.25

def kernel_matrix(points, centers):
    sq_dist = jnp.zeros((points.shape[1], centers.shape[1]), jnp.float32)
    for k in range(3):
        offset = points[k][:, None] - centers[k][None, :]
        sq_dist = sq_dist + offset * offset
    return jnp.exp(-sq_dist)

def deform(template, moment, controls):
    kernel_mat = kernel_matrix(template, controls)
    flat_moment = moment.reshape(moment.shape[0] * 3, moment.shape[2])
    velocity = jnp.dot(flat_moment, kernel_mat.T, precision=precise)
    return template[None] + velocity.reshape(moment.shape[0], 3, template.shape[1])

def elements(vertices, triangles):
    corner_a = jnp.take(vertices, triangles[0], axis=-1)
    corner_b = jnp.take(vertices, triangles[1], axis=-1)
    corner_c = jnp.take(vertices, triangles[2], axis=-1)
    center = (corner_a + corner_b + corner_c) / 3.0
    edge_one = corner_b - corner_a
    edge_two = corner_c - corner_a
    normal = 0.5 * jnp.stack([edge_one[..., 1, :] * edge_two[..., 2, :] - edge_one[..., 2, :] * edge_two[..., 1, :], edge_one[..., 2, :] * edge_two[..., 0, :] - edge_one[..., 0, :] * edge_two[..., 2, :], edge_one[..., 0, :] * edge_two[..., 1, :] - edge_one[..., 1, :] * edge_two[..., 0, :]], axis=-2)
    return (center, normal)

def pair_total(p_cen, u_nor, q_cen, w_nor):
    sq_dist = jnp.float32(0.0)
    inner_prod = jnp.float32(0.0)
    for k in range(3):
        offset = p_cen[..., k, :, None] - q_cen[..., k, None, :]
        sq_dist = sq_dist + offset * offset
        inner_prod = inner_prod + u_nor[..., k, :, None] * w_nor[..., k, None, :]
    norm_u = jnp.sqrt(lax.optimization_barrier(jnp.sum(u_nor * u_nor, axis=-2)) + AREA_SQ)
    norm_w = jnp.sqrt(lax.optimization_barrier(jnp.sum(w_nor * w_nor, axis=-2)) + AREA_SQ)
    values = jnp.exp(-sq_dist) * inner_prod * inner_prod / (norm_u[..., :, None] * norm_w[..., None, :])
    return lax.optimization_barrier(jnp.sum(values, axis=(-2, -1)))

def reference(template_verts, template_tris, local_pairs, partner_blocks, controls, momenta, target_verts, target_tris):
    offsets = (jnp.arange(VERTS, dtype=jnp.int32) // ELEMS * ELEMS)[None]
    global_tris = template_tris + offsets
    bit_count = SHARDS.bit_length() - 1
    block_ids = jnp.arange(BLOCKS, dtype=jnp.int32)
    shard_base = block_ids // BLK_DEV * BLK_DEV
    local_ids = shard_base[:, None] + jnp.arange(BLK_DEV, dtype=jnp.int32)[None]
    partner_ids = [(block_ids // BLK_DEV ^ 1 << r % bit_count) * BLK_DEV + partner_blocks[r] for r in range(4)]
    pair_mask = local_pairs.astype(jnp.float32)

    def to_blocks(array_in):
        return array_in.reshape(3, BLOCKS, BLK).transpose(1, 0, 2)

    def subject_energy(vertices, target_v, target_t):
        center, normal = elements(vertices, global_tris)
        centers, normals = (to_blocks(center), to_blocks(normal))
        t_center, t_normal = elements(target_v, target_t + offsets)
        target_c, target_n = (to_blocks(t_center), to_blocks(t_normal))
        local_sum = pair_total(centers[:, None], normals[:, None], centers[local_ids], normals[local_ids])
        energy_sum = jnp.sum(local_sum * pair_mask)
        for r in range(4):
            energy_sum = energy_sum + jnp.sum(pair_total(centers, normals, centers[partner_ids[r]], normals[partner_ids[r]]))
        energy_sum = energy_sum - 2.0 * jnp.sum(pair_total(centers, normals, target_c, target_n))
        return energy_sum / BLK
    checked = jax.checkpoint(subject_energy)

    def total_loss(template, moment):
        deformed = deform(template, moment, controls)
        energies = lax.map(lambda subject_item: checked(subject_item[0], subject_item[1], subject_item[2]), (deformed, target_verts, target_tris))
        return jnp.sum(energies)
    gradients = jax.grad(total_loss, argnums=(0, 1))(template_verts, momenta)
    return (gradients[0] / SUBJ, gradients[1])
```

```python
import functools
import math

import jax
import jax.numpy as jnp
from jax import lax
from jax.experimental import pallas as pl
from jax.experimental.pallas import tpu as pltpu
from jax.sharding import PartitionSpec as P

AREA_SQ = 0.25
SCALE = math.sqrt(math.log2(math.e))
LANES = 128
ROWS = 16
MESH = pl.DeviceIdType.MESH
f32, bf16 = jnp.float32, jnp.bfloat16
NT = (((1,), (1,)), ((), ()))
NN = (((1,), (0,)), ((), ()))


def split(value):
    high = value.astype(bf16)
    return high, (value - high.astype(f32)).astype(bf16)


def mxu(a, b, dims):
    return lax.dot_general(a, b, dims, preferred_element_type=f32)


def pick_lanes(halves, indices):
    out = []
    for idx in indices:
        low = idx & (LANES - 1)
        value = jnp.take_along_axis(halves[0], low, axis=1, mode="promise_in_bounds")
        for h in range(1, len(halves)):
            other = jnp.take_along_axis(halves[h], low, axis=1, mode="promise_in_bounds")
            value = jnp.where(idx >= h * LANES, other, value)
        out.append(value)
    return out


def cross(a, b):
    return [
        a[1] * b[2] - a[2] * b[1],
        a[2] * b[0] - a[0] * b[2],
        a[0] * b[1] - a[1] * b[0],
    ]


def edges(verts, corner_ids):
    corners = [[pick_lanes(verts[d], corner_ids[k]) for d in range(3)] for k in range(3)]
    pieces = []
    for h in range(len(corner_ids[0])):
        a, b, c = [[corners[k][d][h] for d in range(3)] for k in range(3)]
        center = [(a[d] + b[d] + c[d]) * (1.0 / 3.0) for d in range(3)]
        one = [b[d] - a[d] for d in range(3)]
        two = [c[d] - a[d] for d in range(3)]
        normal = [0.5 * v for v in cross(one, two)]
        pieces.append((center, one, two, normal))
    return pieces


def root_norm(normal):
    return jnp.sqrt(normal[0] * normal[0] + normal[1] * normal[1] + normal[2] * normal[2] + AREA_SQ)


def kernel(
    cfg,
    x_hbm, tris_hbm, local_hbm, partner_hbm, ctrl_hbm, mom_hbm, tv_hbm, tt_hbm,
    tg_out, mg_hbm,
    x_ref, tris_ref, local_ref, partner_ref, ctrl_ref, mom, tv, tt, xs, xl, csc, khi, klo, khi_b, klo_b, bhi, blo, vel, own, tgt, mates, stk, uw, pb, inn, t_hi, t_lo, gout, geo, hot, cots, mg, tgs,
    mom_sem, t_sem, xs_s, xs_r, pn_s, pn_r, ct_s, ct_r, tg_s, tg_r, out_sem,
):
    n, nsub, subjects, elems, ctrl, cdev, bits, chunk = cfg
    rows = 3 * subjects
    halves = elems // LANES
    groups = subjects // 8
    me = lax.axis_index("blk")
    sub = lax.axis_index("subj")

    loads = [
        pltpu.make_async_copy(x_hbm, x_ref, mom_sem.at[0]),
        pltpu.make_async_copy(ctrl_hbm, ctrl_ref, mom_sem.at[1]),
        pltpu.make_async_copy(mom_hbm, mom, mom_sem.at[2]),
    ]
    tloads = [
        pltpu.make_async_copy(tris_hbm, tris_ref, t_sem.at[0]),
        pltpu.make_async_copy(tv_hbm, tv, t_sem.at[1]),
        pltpu.make_async_copy(tt_hbm, tt, t_sem.at[2]),
        pltpu.make_async_copy(local_hbm, local_ref, t_sem.at[3]),
        pltpu.make_async_copy(partner_hbm, partner_ref, t_sem.at[4]),
    ]
    for c in loads + tloads:
        c.start()

    def over_rows(value):
        return jnp.sum(value, axis=0, keepdims=True)

    barrier = pltpu.get_barrier_semaphore()
    for o in range(1, n):
        pl.semaphore_signal(barrier, inc=1, device_id={"blk": me ^ o}, device_id_type=MESH)
    for o in range(1, nsub):
        pl.semaphore_signal(
            barrier, inc=1, device_id={"subj": lax.rem(sub + o, nsub)}, device_id_type=MESH
        )

    def augment(points, near, factor):
        scaled = points * SCALE
        square = over_rows(scaled * scaled)
        ones = jnp.full_like(square, near)
        pair = [ones, square * near] if near < 0 else [square, ones]
        rest = jnp.zeros((3, points.shape[1]), f32)
        return jnp.concatenate([scaled * factor] + pair + [rest], axis=0)

    def thirds(value):
        one = value.astype(bf16).astype(f32)
        two = (value - one).astype(bf16).astype(f32)
        return one, two, value - one - two

    def spread(points, slot):
        b1, b2, b3 = thirds(augment(points, -1.0, 2.0))
        xl[slot] = jnp.concatenate([b1, b1, b2, b2, b1, b3], axis=0).T.astype(bf16)

    loads[0].wait()
    spread(x_ref[...], 0)
    loads[1].wait()
    for i in range(0, ctrl, 1024):
        here = slice(i, i + 1024)
        a1, a2, a3 = thirds(augment(ctrl_ref[:, here], 1.0, 1.0))
        csc[:, here] = jnp.concatenate([a1, a2, a1, a2, a3, a1], axis=0).astype(bf16)
    vel[...] = jnp.zeros_like(vel)

    def kernel_chunk(slot, start, hi_to, lo_to):
        power = mxu(xl[slot], csc[:, pl.ds(start, chunk)], NN)
        hi, lo = split(jnp.exp2(power))
        hi_to[...] = hi
        lo_to[...] = lo

    loads[2].wait()

    def weigh(start, hi_from, lo_from):
        m = mom[:, pl.ds(start, chunk)]
        weighted = [m]
        for d in range(3):
            weighted.append(m * ctrl_ref[d : d + 1, pl.ds(start, chunk)])
        pairs = [split(w) for w in weighted]
        hi = jnp.concatenate([p[0] for p in pairs], axis=0)
        both = mxu(jnp.concatenate([hi] + [p[1] for p in pairs], axis=0), hi_from[...], NT)
        vel[...] += both[0 : 4 * rows] + both[4 * rows :] + mxu(hi, lo_from[...], NT)

    at = lambda i: pl.multiple_of(i * chunk, chunk)
    steps = ctrl // chunk
    kernel_chunk(0, 0, khi, klo)

    def forward(i, carry):
        kernel_chunk(0, at(2 * i + 1), khi_b, klo_b)
        weigh(at(2 * i), khi, klo)
        kernel_chunk(0, at(jnp.minimum(2 * i + 2, steps - 1)), khi, klo)
        weigh(at(2 * i + 1), khi_b, klo_b)
        return carry

    lax.fori_loop(0, steps // 2, forward, 0)

    pl.semaphore_wait(barrier, n - 1 + nsub - 1)

    def to_blk(src, dst, ssem, rsem, o, s):
        return pltpu.make_async_remote_copy(
            src_ref=src, dst_ref=dst, send_sem=ssem.at[s], recv_sem=rsem.at[s],
            device_id={"blk": me ^ o}, device_id_type=MESH,
        )

    x_sends = [to_blk(x_ref, xs.at[o - 1], xs_s, xs_r, o, o - 1) for o in range(1, n)]
    for c in x_sends:
        c.start()

    tloads[0].wait()
    lane = lambda h: slice(h * LANES, (h + 1) * LANES)
    for g in range(groups):
        verts = [
            [
                x_ref[d : d + 1, lane(h)] + vel[pl.ds(d * subjects + g * 8, 8), lane(h)]
                for h in range(halves)
            ]
            for d in range(3)
        ]
        ids = [
            [jnp.broadcast_to(tris_ref[k : k + 1, lane(h)], (8, LANES)) for h in range(halves)]
            for k in range(3)
        ]
        for h, (center, one, two, normal) in enumerate(edges(verts, ids)):
            nu = root_norm(normal)
            inv = 1.0 / jnp.sqrt(nu)
            for d in range(3):
                own[d, g, h] = center[d] * SCALE
                own[3 + d, g, h] = normal[d] * inv
                geo[d, g, h] = one[d]
                geo[3 + d, g, h] = two[d]
                geo[6 + d, g, h] = normal[d]
            geo[9, g, h] = nu

    p_sends = [to_blk(own, mates.at[b], pn_s, pn_r, 2**b, b) for b in range(bits)]
    for c in p_sends:
        c.start()

    for c in tloads[1:]:
        c.wait()
    for g in range(groups):
        part = lambda d: pl.ds(d * subjects + g * 8, 8)
        verts = [[tv[part(d), lane(h)] for h in range(halves)] for d in range(3)]
        ids = [[tt[part(k), lane(h)] for h in range(halves)] for k in range(3)]
        for h, (center, one, two, normal) in enumerate(edges(verts, ids)):
            inv = 1.0 / jnp.sqrt(root_norm(normal))
            for d in range(3):
                tgt[d, g, h] = center[d] * SCALE
                tgt[3 + d, g, h] = normal[d] * inv

    for k in range(3):
        vertex = lax.broadcasted_iota(jnp.int32, (elems, elems), 0)
        hot[:, k * elems : (k + 1) * elems] = jnp.where(
            vertex == tris_ref[k : k + 1, :], 1.0, 0.0
        ).astype(bf16)

    every = list(range(halves))
    as_float = lambda v: v.astype(f32)

    def stack(src, q, w, g, h):
        products = [w[d] * q[k] for d in range(3) for k in range(3)]
        for r, value in enumerate(w + products + q + [jnp.zeros_like(q[0])]):
            stk[src, h, pl.ds(g * 8 * ROWS + r, 8, stride=ROWS), :] = value

    for g in range(groups):
        for h in every:
            stack(0, [own[d, g, h] for d in range(3)], [own[3 + d, g, h] for d in range(3)], g, h)
            stack(1, [tgt[d, g, h] for d in range(3)], [tgt[3 + d, g, h] for d in range(3)], g, h)

    wide = lambda parts: jnp.concatenate(parts, axis=1) if len(parts) > 1 else parts[0]
    first = lambda s: s * ROWS if isinstance(s, int) else pl.multiple_of(s * ROWS, ROWS)
    width_of = lambda blocks: slice(0, len(blocks) * LANES)

    def rows_of(s, src, blocks):
        return [stk[src, b, pl.ds(first(s), ROWS), :] for b in blocks]

    def multiply(s, slot, items):
        for x, (src, tasks) in enumerate(items):
            for own_rows, blocks, _ in tasks:
                hi, lo = split(wide(rows_of(s, src, blocks)))
                inn[slot, x, own_rows, width_of(blocks)] = mxu(
                    uw[s, own_rows, :], jnp.concatenate([hi, lo, hi, lo], axis=0), NN
                )

    def weigh_pairs(s, slot, items):
        for x, (src, tasks) in enumerate(items):
            for own_rows, blocks, _ in tasks:
                for r in range(own_rows.start, own_rows.stop, 32):
                    here = slice(r, r + 32)
                    total = None
                    for d in range(3):
                        q = wide([stk[src, b, pl.ds(first(s) + 12 + d, 1), :] for b in blocks])
                        off = wide([pb[s, d, here, :]] * len(blocks)) - q
                        total = off * off if total is None else total + off * off
                    t = jnp.exp2(-total) * inn[slot, x, here, width_of(blocks)]
                    hi, lo = split(t)
                    t_hi[slot, x, here, width_of(blocks)] = hi
                    t_lo[slot, x, here, width_of(blocks)] = lo

    def collect(s, slot, items, to):
        totals = [None] * halves
        for x, (src, tasks) in enumerate(items):
            for own_rows, blocks, coefs in tasks:
                parts = rows_of(s, src, blocks)
                for a in every:
                    if not own_rows.start <= a * LANES < own_rows.stop:
                        continue
                    hi, lo = split(wide([part * c for part, c in zip(parts, coefs[a])]))
                    both = mxu(
                        jnp.concatenate([hi, lo], axis=0),
                        t_hi[slot, x, lane(a), width_of(blocks)], NT,
                    )
                    term = both[0:ROWS] + both[ROWS:]
                    term = term + mxu(hi, t_lo[slot, x, lane(a), width_of(blocks)], NT)
                    totals[a] = term if totals[a] is None else totals[a] + term
        for a in every:
            gout[to, a, pl.ds(first(s), ROWS), :] = totals[a]

    def sweep(items, to, start, stop, ahead=None):
        last = stop - 1

        def pair(i, carry):
            x = start + 2 * i
            collect(jnp.maximum(x - 1, start), 1, items, to)
            weigh_pairs(x, 0, items)
            multiply(x + 1, 1, items)
            collect(x, 0, items, to)
            weigh_pairs(x + 1, 1, items)
            multiply(jnp.minimum(x + 2, last), 0, items)
            if ahead is not None:
                ahead(jnp.minimum(x + 3, last))
                ahead(jnp.minimum(x + 4, last))
            return carry

        if ahead is not None:
            for s in range(3):
                ahead(start + s)
        multiply(start, 0, items)
        lax.fori_loop(0, (stop - start) // 2, pair, 0)
        collect(last, 1, items, to)

    def prepare(s):
        row = lax.broadcasted_iota(jnp.int32, (ROWS, LANES), 0)
        for a in every:
            mine = stk[0, a, pl.ds(first(s), ROWS), :]
            weights = jnp.where(row < 3, mine, 0.0)
            hi = weights.astype(bf16).astype(f32)
            lo = weights - hi
            columns = jnp.concatenate([hi, hi, lo, lo, mine], axis=0).T
            uw[s, lane(a), :] = columns[:, 0 : 4 * ROWS].astype(bf16)
            for d in range(3):
                at_d = 4 * ROWS + 12 + d
                pb[s, d, lane(a), :] = jnp.broadcast_to(columns[:, at_d : at_d + 1], (LANES, LANES))

    whole = slice(0, elems)
    local = {a: [as_float(local_ref[a, b] + local_ref[b, a]) for b in every] for a in every}
    near = [(0, [(whole, every, local)])]
    near.append((1, [(lane(a), [a], {a: [-2.0]}) for a in every]))
    sweep(near, 0, 0, subjects, prepare)

    distant = []
    for bit in range(bits):
        p_sends[bit].wait_recv()
        for g in range(groups):
            for h in every:
                take = lambda d: mates[bit, d, g, h]
                stack(2 + bit, [take(d) for d in range(3)], [take(3 + d) for d in range(3)], g, h)
        coefs = {a: [] for a in every}
        for a in every:
            for b in every:
                count = jnp.int32(0)
                for r in range(4):
                    if r % (n.bit_length() - 1) == bit:
                        count = count + jnp.where(partner_ref[a, r] == b, 2, 0)
                coefs[a].append(as_float(count))
        distant.append((2 + bit, [(whole, every, coefs)]))

    width = 1.0 / LANES
    pack = 3 * 8

    def halve(value):
        hi = value.astype(bf16).astype(f32)
        return jnp.concatenate([hi, value - hi], axis=0).astype(bf16)

    def finish(g):
        corner = [[[None] * halves for _ in range(3)] for _ in range(3)]
        for h in range(halves):
            one = [geo[d, g, h] for d in range(3)]
            two = [geo[3 + d, g, h] for d in range(3)]
            u = [geo[6 + d, g, h] for d in range(3)]
            inv = 1.0 / geo[9, g, h]
            root = jnp.sqrt(geo[9, g, h])
            part = lambda i, r: gout[i, h, pl.ds(g * 8 * ROWS + r, 8, stride=ROWS), :]
            take = lambda r: part(0, r) + part(1, r)
            turned = [root * take(d) for d in range(3)]
            total = u[0] * turned[0] + u[1] * turned[1] + u[2] * turned[2]
            moved = []
            for k in range(3):
                mixed = [u[d] * take(3 + 3 * d + k) for d in range(3)]
                moved.append(own[k, g, h] * total - root * (mixed[0] + mixed[1] + mixed[2]))
            shrink = inv * inv * inv * total
            gp = [moved[d] * inv * (-2.0 * width / SCALE / 3.0) for d in range(3)]
            gu = [(2.0 * inv * turned[d] - u[d] * shrink) * (0.5 * width) for d in range(3)]
            g_one = cross(two, gu)
            g_two = cross(gu, one)
            for d in range(3):
                corner[0][d][h] = gp[d] - g_one[d] - g_two[d]
                corner[1][d][h] = gp[d] + g_one[d]
                corner[2][d][h] = gp[d] + g_two[d]
        value = jnp.concatenate(
            [
                jnp.concatenate([corner[k][d][h] for d in range(3)], axis=0)
                for k in range(3)
                for h in range(halves)
            ],
            axis=1,
        )
        both = mxu(halve(value), hot[...], NT)
        cots[0, g] = both[0:pack] + both[pack:]

    c_sends = []
    for g in range(groups):
        sweep(distant, 1, g * 8, g * 8 + 8)
        finish(g)
        for o in range(1, n):
            at_g = g * (n - 1) + o - 1
            c_sends.append(to_blk(cots.at[0, g], cots.at[o, g], ct_s, ct_r, o, at_g))
            c_sends[-1].start()

    def vel_of(c, g):
        base = c * rows + g * 8
        return jnp.concatenate([vel[pl.ds(base + d * subjects, 8), :] for d in range(3)], axis=0)

    factor = 1.0 / (subjects * nsub)
    over_groups = lambda f: sum(over_rows(f(g, cots[0, g])) for g in range(groups))
    plain = over_groups(lambda g, cot: cot * vel_of(0, g))
    for d in range(3):
        direct = over_groups(lambda g, cot: cot[d * 8 : (d + 1) * 8])
        moved = over_groups(lambda g, cot: cot * vel_of(d + 1, g))
        tgs[sub, pl.ds(d, 1), :] = factor * (direct - 2.0 * (x_ref[d : d + 1, :] * plain - moved))

    g_sends = []
    for o in range(1, nsub):
        g_sends.append(
            pltpu.make_async_remote_copy(
                src_ref=tgs.at[sub], dst_ref=tgs.at[sub], send_sem=tg_s.at[o - 1],
                recv_sem=tg_r.at[o - 1], device_id={"subj": lax.rem(sub + o, nsub)},
                device_id_type=MESH,
            )
        )
    for c in g_sends:
        c.start()

    for o in range(1, n):
        x_sends[o - 1].wait_recv()
        spread(xs[o - 1], o)

    def backward(make, uses):
        lhs = [halve(cots[o, g]) for o, g in uses]

        def body(i, carry):
            here = pl.ds(at(i), chunk)
            if make is not None:
                start = pl.multiple_of(me * cdev + i * chunk, chunk)
                kernel_chunk(make, start, bhi.at[make, :, here], blo.at[make, :, here])
            sums = {}
            for (o, g), two in zip(uses, lhs):
                both = mxu(two, bhi[o, :, here], NN) + mxu(two, blo[o, :, here], NN)
                term = both[0:pack] + both[pack:]
                sums[g] = sums[g] + term if g in sums else term
            for g, term in sums.items():
                fresh = (0, g) in uses
                for d in range(3):
                    piece = term[d * 8 : (d + 1) * 8]
                    block = pl.ds(d * subjects + g * 8, 8)
                    mg[block, here] = piece if fresh else mg[block, here] + piece
            return carry

        lax.fori_loop(0, cdev // chunk, body, 0)

    every_g = list(range(groups))
    early, late = every_g[:-1], every_g[-1]
    backward(0, [])
    backward(1, [(0, g) for g in every_g])
    for g in early:
        for o in range(1, n):
            c_sends[g * (n - 1) + o - 1].wait_recv()
    for o in range(1, n):
        backward(o + 1 if o + 1 < n else None, [(o, g) for g in early])
    for o in range(1, n):
        c_sends[late * (n - 1) + o - 1].wait_recv()
        backward(None, [(o, late)])

    outs = [pltpu.make_async_copy(mg, mg_hbm, out_sem.at[0])]
    for c in outs:
        c.start()
    for c in g_sends:
        c.wait_recv()
    tg_sum = tgs[0]
    for o in range(1, nsub):
        tg_sum = tg_sum + tgs[o]
    tg_out[...] = tg_sum
    for c in x_sends + p_sends + c_sends + g_sends:
        c.wait_send()
    for c in outs:
        c.wait()


def on_device(n, nsub, tverts, ttris, local, partner, controls, momenta, tv, tt):
    subjects, _, ctrl = momenta.shape
    elems = tverts.shape[1]
    halves = elems // LANES
    groups = subjects // 8
    rows = 3 * subjects
    cdev = ctrl // n
    bits = min(4, n.bit_length() - 1)
    chunk = min(512, cdev)
    cfg = (n, nsub, subjects, elems, ctrl, cdev, bits, chunk)
    vmem = pl.BlockSpec(memory_space=pltpu.VMEM)
    hbm = pl.BlockSpec(memory_space=pltpu.HBM)
    panel = (6, groups, halves, 8, LANES)
    dma = pltpu.SemaphoreType.DMA
    by_axis = lambda v: v.transpose(1, 0, 2).reshape(rows, v.shape[2])
    template_grad, grads = pl.pallas_call(
        functools.partial(kernel, cfg),
        out_shape=(
            jax.ShapeDtypeStruct((3, elems), f32),
            jax.ShapeDtypeStruct((rows, cdev), f32),
        ),
        in_specs=[hbm] * 8,
        out_specs=(vmem, hbm),
        scratch_shapes=[
            pltpu.VMEM((3, elems), f32),
            pltpu.VMEM((3, elems), jnp.int32),
            pltpu.SMEM(local.shape, jnp.int32),
            pltpu.SMEM(partner.shape[::-1], jnp.int32),
            pltpu.VMEM((3, ctrl), f32),
            pltpu.VMEM((rows, ctrl), f32),
            pltpu.VMEM((rows, elems), f32),
            pltpu.VMEM((rows, elems), jnp.int32),
            pltpu.VMEM((n - 1, 3, elems), f32),
            pltpu.VMEM((n, elems, 48), bf16),
            pltpu.VMEM((48, ctrl), bf16),
            pltpu.VMEM((elems, chunk), bf16),
            pltpu.VMEM((elems, chunk), bf16),
            pltpu.VMEM((elems, chunk), bf16),
            pltpu.VMEM((elems, chunk), bf16),
            pltpu.VMEM((n, elems, cdev), bf16),
            pltpu.VMEM((n, elems, cdev), bf16),
            pltpu.VMEM((4 * rows, elems), f32),
            pltpu.VMEM(panel, f32),
            pltpu.VMEM(panel, f32),
            pltpu.VMEM((bits,) + panel, f32),
            pltpu.VMEM((2 + bits, halves, subjects * ROWS, LANES), f32),
            pltpu.VMEM((subjects, elems, 4 * ROWS), bf16),
            pltpu.VMEM((subjects, 3, elems, LANES), f32),
            pltpu.VMEM((2, max(2, bits), elems, elems), f32),
            pltpu.VMEM((2, max(2, bits), elems, elems), bf16),
            pltpu.VMEM((2, max(2, bits), elems, elems), bf16),
            pltpu.VMEM((2, halves, subjects * ROWS, LANES), f32),
            pltpu.VMEM((10,) + panel[1:], f32),
            pltpu.VMEM((elems, 3 * elems), bf16),
            pltpu.VMEM((n, groups, 24, elems), f32),
            pltpu.VMEM((rows, cdev), f32),
            pltpu.VMEM((nsub, 3, elems), f32),
            dma((3,)), dma((5,)),
            dma((n - 1,)), dma((n - 1,)),
            dma((bits,)), dma((bits,)),
            dma((groups * (n - 1),)), dma((groups * (n - 1),)),
            dma((nsub - 1,)), dma((nsub - 1,)),
            dma((1,)),
        ],
        compiler_params=pltpu.CompilerParams(
            collective_id=0, has_side_effects=True, vmem_limit_bytes=64 * 2**20
        ),
        name="atlas",
    )(tverts, ttris, local, partner.T, controls, by_axis(momenta), by_axis(tv), by_axis(tt))
    return template_grad, grads.reshape(3, subjects, cdev).transpose(1, 0, 2)


def solution(mesh):
    return jax.shard_map(
        functools.partial(on_device, mesh.shape["blk"], mesh.shape["subj"]),
        mesh=mesh,
        in_specs=(
            P(None, ("groups", "blk")),
            P(None, ("groups", "blk")),
            P("blk", None),
            P(None, "blk"),
            P(),
            P(("groups", "subj"), None, None),
            P(("groups", "subj"), None, "blk"),
            P(("groups", "subj"), None, "blk"),
        ),
        out_specs=(P(None, ("groups", "blk")), P(("groups", "subj"), None, "blk")),
        check_vma=False,
    )
```

```python
import functools
import math

import jax
import jax.numpy as jnp
from jax import lax
from jax.experimental import pallas as pl
from jax.experimental.pallas import tpu as pltpu
from jax.sharding import PartitionSpec as P

AREA_SQ = 0.25
SCALE = math.sqrt(math.log2(math.e))
LANES = 128
ROWS = 16
MESH = pl.DeviceIdType.MESH
f32, bf16 = jnp.float32, jnp.bfloat16
NT = (((1,), (1,)), ((), ()))
NN = (((1,), (0,)), ((), ()))


def split(value):
    high = value.astype(bf16)
    return high, (value - high.astype(f32)).astype(bf16)


def mxu(a, b, dims):
    return lax.dot_general(a, b, dims, preferred_element_type=f32)


def pick_lanes(halves, indices):
    out = []
    for idx in indices:
        low = idx & (LANES - 1)
        value = jnp.take_along_axis(halves[0], low, axis=1, mode="promise_in_bounds")
        for h in range(1, len(halves)):
            other = jnp.take_along_axis(halves[h], low, axis=1, mode="promise_in_bounds")
            value = jnp.where(idx >= h * LANES, other, value)
        out.append(value)
    return out


def cross(a, b):
    return [
        a[1] * b[2] - a[2] * b[1],
        a[2] * b[0] - a[0] * b[2],
        a[0] * b[1] - a[1] * b[0],
    ]


def edges(verts, corner_ids):
    corners = [[pick_lanes(verts[d], corner_ids[k]) for d in range(3)] for k in range(3)]
    pieces = []
    for h in range(len(corner_ids[0])):
        a, b, c = [[corners[k][d][h] for d in range(3)] for k in range(3)]
        center = [(a[d] + b[d] + c[d]) * (1.0 / 3.0) for d in range(3)]
        one = [b[d] - a[d] for d in range(3)]
        two = [c[d] - a[d] for d in range(3)]
        normal = [0.5 * v for v in cross(one, two)]
        pieces.append((center, one, two, normal))
    return pieces


def root_norm(normal):
    return jnp.sqrt(normal[0] * normal[0] + normal[1] * normal[1] + normal[2] * normal[2] + AREA_SQ)


def kernel(
    cfg,
    x_hbm, tris_hbm, local_hbm, partner_hbm, ctrl_hbm, mom_hbm, tv_hbm, tt_hbm,
    tg_out, mg_hbm,
    x_ref, tris_ref, local_ref, partner_ref, ctrl_ref, mom, tv, tt, xs, xl, csc, khi, klo, khi_b, klo_b, bhi, blo, vel, own, tgt, mates, stk, uw, pb, inn, t_hi, t_lo, gout, geo, hot, cots, mg, tgs,
    mom_sem, t_sem, xs_s, xs_r, pn_s, pn_r, ct_s, ct_r, tg_s, tg_r, out_sem,
):
    n, nsub, subjects, elems, ctrl, cdev, bits, chunk = cfg
    rows = 3 * subjects
    halves = elems // LANES
    groups = subjects // 8
    me = lax.axis_index("blk")
    sub = lax.axis_index("subj")

    loads = [
        pltpu.make_async_copy(x_hbm, x_ref, mom_sem.at[0]),
        pltpu.make_async_copy(ctrl_hbm, ctrl_ref, mom_sem.at[1]),
        pltpu.make_async_copy(mom_hbm, mom, mom_sem.at[2]),
    ]
    tloads = [
        pltpu.make_async_copy(tris_hbm, tris_ref, t_sem.at[0]),
        pltpu.make_async_copy(tv_hbm, tv, t_sem.at[1]),
        pltpu.make_async_copy(tt_hbm, tt, t_sem.at[2]),
        pltpu.make_async_copy(local_hbm, local_ref, t_sem.at[3]),
        pltpu.make_async_copy(partner_hbm, partner_ref, t_sem.at[4]),
    ]
    for c in loads + tloads:
        c.start()

    def over_rows(value):
        return jnp.sum(value, axis=0, keepdims=True)

    barrier = pltpu.get_barrier_semaphore()
    for o in range(1, n):
        pl.semaphore_signal(barrier, inc=1, device_id={"blk": me ^ o}, device_id_type=MESH)
    for o in range(1, nsub):
        pl.semaphore_signal(
            barrier, inc=1, device_id={"subj": lax.rem(sub + o, nsub)}, device_id_type=MESH
        )

    def augment(points, near, factor):
        scaled = points * SCALE
        square = over_rows(scaled * scaled)
        ones = jnp.full_like(square, near)
        pair = [ones, square * near] if near < 0 else [square, ones]
        rest = jnp.zeros((3, points.shape[1]), f32)
        return jnp.concatenate([scaled * factor] + pair + [rest], axis=0)

    def thirds(value):
        one = value.astype(bf16).astype(f32)
        two = (value - one).astype(bf16).astype(f32)
        return one, two, value - one - two

    def spread(points, slot):
        b1, b2, b3 = thirds(augment(points, -1.0, 2.0))
        xl[slot] = jnp.concatenate([b1, b1, b2, b2, b1, b3], axis=0).T.astype(bf16)

    loads[0].wait()
    spread(x_ref[...], 0)
    loads[1].wait()
    for i in range(0, ctrl, 1024):
        here = slice(i, i + 1024)
        a1, a2, a3 = thirds(augment(ctrl_ref[:, here], 1.0, 1.0))
        csc[:, here] = jnp.concatenate([a1, a2, a1, a2, a3, a1], axis=0).astype(bf16)
    vel[...] = jnp.zeros_like(vel)

    def kernel_chunk(slot, start, hi_to, lo_to):
        power = mxu(xl[slot], csc[:, pl.ds(start, chunk)], NN)
        hi, lo = split(jnp.exp2(power))
        hi_to[...] = hi
        lo_to[...] = lo

    loads[2].wait()

    def weigh(start, hi_from, lo_from):
        m = mom[:, pl.ds(start, chunk)]
        weighted = [m]
        for d in range(3):
            weighted.append(m * ctrl_ref[d : d + 1, pl.ds(start, chunk)])
        pairs = [split(w) for w in weighted]
        hi = jnp.concatenate([p[0] for p in pairs], axis=0)
        both = mxu(jnp.concatenate([hi] + [p[1] for p in pairs], axis=0), hi_from[...], NT)
        vel[...] += both[0 : 4 * rows] + both[4 * rows :] + mxu(hi, lo_from[...], NT)

    own_chunks = cdev // chunk
    main = ctrl // chunk - own_chunks
    span = lambda c: slice(c * chunk, (c + 1) * chunk)

    def where(j):
        return pl.multiple_of(lax.rem((me + 1) * cdev + j * chunk, ctrl), chunk)

    now, later = (khi, klo), (khi_b, klo_b)
    kernel_chunk(0, where(0), *now)
    odd = main % 2
    if odd:
        kernel_chunk(0, where(1), *later)
        weigh(where(0), *now)
        now, later = later, now

    def forward(i, carry):
        j = odd + 2 * i
        kernel_chunk(0, where(j + 1), *later)
        weigh(where(j), *now)
        kernel_chunk(0, where(j + 2), *now)
        weigh(where(j + 1), *later)
        return carry

    lax.fori_loop(0, main // 2, forward, 0)
    bhi[0, :, span(0)] = now[0][...]
    blo[0, :, span(0)] = now[1][...]
    for c in range(own_chunks):
        if c + 1 < own_chunks:
            kernel_chunk(0, where(main + c + 1), bhi.at[0, :, span(c + 1)], blo.at[0, :, span(c + 1)])
        weigh(where(main + c), *(now if c == 0 else (bhi.at[0, :, span(c)], blo.at[0, :, span(c)])))

    pl.semaphore_wait(barrier, n - 1 + nsub - 1)

    def to_blk(src, dst, ssem, rsem, o, s):
        return pltpu.make_async_remote_copy(
            src_ref=src, dst_ref=dst, send_sem=ssem.at[s], recv_sem=rsem.at[s],
            device_id={"blk": me ^ o}, device_id_type=MESH,
        )

    x_sends = [to_blk(x_ref, xs.at[o - 1], xs_s, xs_r, o, o - 1) for o in range(1, n)]
    for c in x_sends:
        c.start()

    tloads[0].wait()
    lane = lambda h: slice(h * LANES, (h + 1) * LANES)
    for g in range(groups):
        verts = [
            [
                x_ref[d : d + 1, lane(h)] + vel[pl.ds(d * subjects + g * 8, 8), lane(h)]
                for h in range(halves)
            ]
            for d in range(3)
        ]
        ids = [
            [jnp.broadcast_to(tris_ref[k : k + 1, lane(h)], (8, LANES)) for h in range(halves)]
            for k in range(3)
        ]
        for h, (center, one, two, normal) in enumerate(edges(verts, ids)):
            nu = root_norm(normal)
            inv = 1.0 / jnp.sqrt(nu)
            for d in range(3):
                own[d, g, h] = center[d] * SCALE
                own[3 + d, g, h] = normal[d] * inv
                geo[d, g, h] = one[d]
                geo[3 + d, g, h] = two[d]
                geo[6 + d, g, h] = normal[d]
            geo[9, g, h] = nu

    p_sends = [to_blk(own, mates.at[b], pn_s, pn_r, 2**b, b) for b in range(bits)]
    for c in p_sends:
        c.start()

    for c in tloads[1:]:
        c.wait()
    for g in range(groups):
        part = lambda d: pl.ds(d * subjects + g * 8, 8)
        verts = [[tv[part(d), lane(h)] for h in range(halves)] for d in range(3)]
        ids = [[tt[part(k), lane(h)] for h in range(halves)] for k in range(3)]
        for h, (center, one, two, normal) in enumerate(edges(verts, ids)):
            inv = 1.0 / jnp.sqrt(root_norm(normal))
            for d in range(3):
                tgt[d, g, h] = center[d] * SCALE
                tgt[3 + d, g, h] = normal[d] * inv

    for k in range(3):
        vertex = lax.broadcasted_iota(jnp.int32, (elems, elems), 0)
        hot[:, k * elems : (k + 1) * elems] = jnp.where(
            vertex == tris_ref[k : k + 1, :], 1.0, 0.0
        ).astype(bf16)

    every = list(range(halves))
    as_float = lambda v: v.astype(f32)

    def stack(src, q, w, g, h):
        products = [w[d] * q[k] for d in range(3) for k in range(3)]
        for r, value in enumerate(w + products + q + [jnp.zeros_like(q[0])]):
            stk[src, h, pl.ds(g * 8 * ROWS + r, 8, stride=ROWS), :] = value

    for g in range(groups):
        for h in every:
            stack(0, [own[d, g, h] for d in range(3)], [own[3 + d, g, h] for d in range(3)], g, h)
            stack(1, [tgt[d, g, h] for d in range(3)], [tgt[3 + d, g, h] for d in range(3)], g, h)

    wide = lambda parts: jnp.concatenate(parts, axis=1) if len(parts) > 1 else parts[0]
    first = lambda s: s * ROWS if isinstance(s, int) else pl.multiple_of(s * ROWS, ROWS)
    width_of = lambda blocks: slice(0, len(blocks) * LANES)

    def rows_of(s, src, blocks):
        return [stk[src, b, pl.ds(first(s), ROWS), :] for b in blocks]

    def multiply(s, slot, items):
        for x, (src, tasks) in enumerate(items):
            for own_rows, blocks, _ in tasks:
                hi, lo = split(wide(rows_of(s, src, blocks)))
                inn[slot, x, own_rows, width_of(blocks)] = mxu(
                    uw[s, own_rows, :], jnp.concatenate([hi, lo, hi, lo], axis=0), NN
                )

    def weigh_pairs(s, slot, items):
        for x, (src, tasks) in enumerate(items):
            for own_rows, blocks, _ in tasks:
                for r in range(own_rows.start, own_rows.stop, 32):
                    here = slice(r, r + 32)
                    total = None
                    for d in range(3):
                        q = wide([stk[src, b, pl.ds(first(s) + 12 + d, 1), :] for b in blocks])
                        off = wide([pb[s, d, here, :]] * len(blocks)) - q
                        total = off * off if total is None else total + off * off
                    t = jnp.exp2(-total) * inn[slot, x, here, width_of(blocks)]
                    hi, lo = split(t)
                    t_hi[slot, x, here, width_of(blocks)] = hi
                    t_lo[slot, x, here, width_of(blocks)] = lo

    def collect(s, slot, items, to):
        totals = [None] * halves
        for x, (src, tasks) in enumerate(items):
            for own_rows, blocks, coefs in tasks:
                parts = rows_of(s, src, blocks)
                for a in every:
                    if not own_rows.start <= a * LANES < own_rows.stop:
                        continue
                    hi, lo = split(wide([part * c for part, c in zip(parts, coefs[a])]))
                    both = mxu(
                        jnp.concatenate([hi, lo], axis=0),
                        t_hi[slot, x, lane(a), width_of(blocks)], NT,
                    )
                    term = both[0:ROWS] + both[ROWS:]
                    term = term + mxu(hi, t_lo[slot, x, lane(a), width_of(blocks)], NT)
                    totals[a] = term if totals[a] is None else totals[a] + term
        for a in every:
            gout[to, a, pl.ds(first(s), ROWS), :] = totals[a]

    def sweep(items, to, start, stop, ahead=None):
        last = stop - 1

        def pair(i, carry):
            x = start + 2 * i
            collect(jnp.maximum(x - 1, start), 1, items, to)
            weigh_pairs(x, 0, items)
            multiply(x + 1, 1, items)
            collect(x, 0, items, to)
            weigh_pairs(x + 1, 1, items)
            multiply(jnp.minimum(x + 2, last), 0, items)
            if ahead is not None:
                ahead(jnp.minimum(x + 3, last))
                ahead(jnp.minimum(x + 4, last))
            return carry

        if ahead is not None:
            for s in range(3):
                ahead(start + s)
        multiply(start, 0, items)
        lax.fori_loop(0, (stop - start) // 2, pair, 0)
        collect(last, 1, items, to)

    def prepare(s):
        row = lax.broadcasted_iota(jnp.int32, (ROWS, LANES), 0)
        for a in every:
            mine = stk[0, a, pl.ds(first(s), ROWS), :]
            weights = jnp.where(row < 3, mine, 0.0)
            hi = weights.astype(bf16).astype(f32)
            lo = weights - hi
            columns = jnp.concatenate([hi, hi, lo, lo, mine], axis=0).T
            uw[s, lane(a), :] = columns[:, 0 : 4 * ROWS].astype(bf16)
            for d in range(3):
                at_d = 4 * ROWS + 12 + d
                pb[s, d, lane(a), :] = jnp.broadcast_to(columns[:, at_d : at_d + 1], (LANES, LANES))

    whole = slice(0, elems)
    local = {a: [as_float(local_ref[a, b] + local_ref[b, a]) for b in every] for a in every}
    near = [(0, [(whole, every, local)])]
    near.append((1, [(lane(a), [a], {a: [-2.0]}) for a in every]))
    sweep(near, 0, 0, subjects, prepare)

    distant = []
    for bit in range(bits):
        p_sends[bit].wait_recv()
        for g in range(groups):
            for h in every:
                take = lambda d: mates[bit, d, g, h]
                stack(2 + bit, [take(d) for d in range(3)], [take(3 + d) for d in range(3)], g, h)
        coefs = {a: [] for a in every}
        for a in every:
            for b in every:
                count = jnp.int32(0)
                for r in range(4):
                    if r % (n.bit_length() - 1) == bit:
                        count = count + jnp.where(partner_ref[a, r] == b, 2, 0)
                coefs[a].append(as_float(count))
        distant.append((2 + bit, [(whole, every, coefs)]))

    width = 1.0 / LANES
    pack = 3 * 8

    def halve(value):
        hi = value.astype(bf16).astype(f32)
        return jnp.concatenate([hi, value - hi], axis=0).astype(bf16)

    def finish(g):
        corner = [[[None] * halves for _ in range(3)] for _ in range(3)]
        for h in range(halves):
            one = [geo[d, g, h] for d in range(3)]
            two = [geo[3 + d, g, h] for d in range(3)]
            u = [geo[6 + d, g, h] for d in range(3)]
            inv = 1.0 / geo[9, g, h]
            root = jnp.sqrt(geo[9, g, h])
            part = lambda i, r: gout[i, h, pl.ds(g * 8 * ROWS + r, 8, stride=ROWS), :]
            take = lambda r: part(0, r) + part(1, r)
            turned = [root * take(d) for d in range(3)]
            total = u[0] * turned[0] + u[1] * turned[1] + u[2] * turned[2]
            moved = []
            for k in range(3):
                mixed = [u[d] * take(3 + 3 * d + k) for d in range(3)]
                moved.append(own[k, g, h] * total - root * (mixed[0] + mixed[1] + mixed[2]))
            shrink = inv * inv * inv * total
            gp = [moved[d] * inv * (-2.0 * width / SCALE / 3.0) for d in range(3)]
            gu = [(2.0 * inv * turned[d] - u[d] * shrink) * (0.5 * width) for d in range(3)]
            g_one = cross(two, gu)
            g_two = cross(gu, one)
            for d in range(3):
                corner[0][d][h] = gp[d] - g_one[d] - g_two[d]
                corner[1][d][h] = gp[d] + g_one[d]
                corner[2][d][h] = gp[d] + g_two[d]
        value = jnp.concatenate(
            [
                jnp.concatenate([corner[k][d][h] for d in range(3)], axis=0)
                for k in range(3)
                for h in range(halves)
            ],
            axis=1,
        )
        both = mxu(halve(value), hot[...], NT)
        cots[0, g] = both[0:pack] + both[pack:]

    c_sends = []
    for g in range(groups):
        sweep(distant, 1, g * 8, g * 8 + 8)
        finish(g)
        for o in range(1, n):
            at_g = g * (n - 1) + o - 1
            c_sends.append(to_blk(cots.at[0, g], cots.at[o, g], ct_s, ct_r, o, at_g))
            c_sends[-1].start()

    def vel_of(c, g):
        base = c * rows + g * 8
        return jnp.concatenate([vel[pl.ds(base + d * subjects, 8), :] for d in range(3)], axis=0)

    factor = 1.0 / (subjects * nsub)
    over_groups = lambda f: sum(over_rows(f(g, cots[0, g])) for g in range(groups))
    plain = over_groups(lambda g, cot: cot * vel_of(0, g))
    for d in range(3):
        direct = over_groups(lambda g, cot: cot[d * 8 : (d + 1) * 8])
        moved = over_groups(lambda g, cot: cot * vel_of(d + 1, g))
        tgs[sub, pl.ds(d, 1), :] = factor * (direct - 2.0 * (x_ref[d : d + 1, :] * plain - moved))

    g_sends = []
    for o in range(1, nsub):
        g_sends.append(
            pltpu.make_async_remote_copy(
                src_ref=tgs.at[sub], dst_ref=tgs.at[sub], send_sem=tg_s.at[o - 1],
                recv_sem=tg_r.at[o - 1], device_id={"subj": lax.rem(sub + o, nsub)},
                device_id_type=MESH,
            )
        )
    for c in g_sends:
        c.start()

    for o in range(1, n):
        x_sends[o - 1].wait_recv()
        spread(xs[o - 1], o)

    for o in range(1, n):
        for c in range(own_chunks):
            start = pl.multiple_of(me * cdev + c * chunk, chunk)
            kernel_chunk(o, start, bhi.at[o, :, span(c)], blo.at[o, :, span(c)])

    outs = []

    def backward(o):
        halves_of = [cots[o, g] for g in range(groups)]
        value = jnp.concatenate(halves_of, axis=0)
        high = value.astype(bf16).astype(f32)
        two = jnp.concatenate([high, value - high], axis=0).astype(bf16)
        high = high.astype(bf16)

        for c in range(own_chunks):
            both = mxu(two, bhi[o, :, span(c)], NN)
            term = both[0:rows] + both[rows:] + mxu(high, blo[o, :, span(c)], NN)
            for g in range(groups):
                for d in range(3):
                    base = g * pack + d * 8
                    piece = term[base : base + 8]
                    block = pl.ds(d * subjects + g * 8, 8)
                    mg[block, span(c)] = mg[block, span(c)] + piece if o else piece
            if o == n - 1:
                outs.append(
                    pltpu.make_async_copy(mg.at[:, span(c)], mg_hbm.at[:, span(c)], out_sem.at[c])
                )
                outs[-1].start()

    backward(0)
    for o in range(1, n):
        for g in range(groups):
            c_sends[g * (n - 1) + o - 1].wait_recv()
        backward(o)

    for c in g_sends:
        c.wait_recv()
    tg_sum = tgs[0]
    for o in range(1, nsub):
        tg_sum = tg_sum + tgs[o]
    tg_out[...] = tg_sum
    for c in x_sends + p_sends + c_sends + g_sends:
        c.wait_send()
    for c in outs:
        c.wait()


def deliver(tg, mg, tg_out, mg_out, tg_held, held, sem_in, sem_out):
    moves = []
    for d in range(3):
        moves.append(
            (
                pltpu.make_async_copy(mg.at[d], held.at[d], sem_in.at[d]),
                pltpu.make_async_copy(held.at[d], mg_out.at[d], sem_out.at[d]),
            )
        )
    moves.append(
        (
            pltpu.make_async_copy(tg, tg_held, sem_in.at[3]),
            pltpu.make_async_copy(tg_held, tg_out, sem_out.at[3]),
        )
    )
    for c in moves:
        c[0].start()
    for c in moves:
        c[0].wait()
        c[1].start()
    for c in moves:
        c[1].wait()


def on_device(n, nsub, tverts, ttris, local, partner, controls, momenta, tv, tt):
    subjects, _, ctrl = momenta.shape
    elems = tverts.shape[1]
    halves = elems // LANES
    groups = subjects // 8
    rows = 3 * subjects
    cdev = ctrl // n
    bits = min(4, n.bit_length() - 1)
    chunk = min(512, cdev)
    cfg = (n, nsub, subjects, elems, ctrl, cdev, bits, chunk)
    vmem = pl.BlockSpec(memory_space=pltpu.VMEM)
    hbm = pl.BlockSpec(memory_space=pltpu.HBM)
    panel = (6, groups, halves, 8, LANES)
    dma = pltpu.SemaphoreType.DMA
    by_axis = lambda v: v.transpose(1, 0, 2).reshape(rows, v.shape[2])
    template_grad, grads = pl.pallas_call(
        functools.partial(kernel, cfg),
        out_shape=(
            jax.ShapeDtypeStruct((3, elems), f32),
            jax.ShapeDtypeStruct((rows, cdev), f32),
        ),
        in_specs=[hbm] * 8,
        out_specs=(vmem, hbm),
        scratch_shapes=[
            pltpu.VMEM((3, elems), f32),
            pltpu.VMEM((3, elems), jnp.int32),
            pltpu.SMEM(local.shape, jnp.int32),
            pltpu.SMEM(partner.shape[::-1], jnp.int32),
            pltpu.VMEM((3, ctrl), f32),
            pltpu.VMEM((rows, ctrl), f32),
            pltpu.VMEM((rows, elems), f32),
            pltpu.VMEM((rows, elems), jnp.int32),
            pltpu.VMEM((n - 1, 3, elems), f32),
            pltpu.VMEM((n, elems, 48), bf16),
            pltpu.VMEM((48, ctrl), bf16),
            pltpu.VMEM((elems, chunk), bf16),
            pltpu.VMEM((elems, chunk), bf16),
            pltpu.VMEM((elems, chunk), bf16),
            pltpu.VMEM((elems, chunk), bf16),
            pltpu.VMEM((n, elems, cdev), bf16),
            pltpu.VMEM((n, elems, cdev), bf16),
            pltpu.VMEM((4 * rows, elems), f32),
            pltpu.VMEM(panel, f32),
            pltpu.VMEM(panel, f32),
            pltpu.VMEM((bits,) + panel, f32),
            pltpu.VMEM((2 + bits, halves, subjects * ROWS, LANES), f32),
            pltpu.VMEM((subjects, elems, 4 * ROWS), bf16),
            pltpu.VMEM((subjects, 3, elems, LANES), f32),
            pltpu.VMEM((2, max(2, bits), elems, elems), f32),
            pltpu.VMEM((2, max(2, bits), elems, elems), bf16),
            pltpu.VMEM((2, max(2, bits), elems, elems), bf16),
            pltpu.VMEM((2, halves, subjects * ROWS, LANES), f32),
            pltpu.VMEM((10,) + panel[1:], f32),
            pltpu.VMEM((elems, 3 * elems), bf16),
            pltpu.VMEM((n, groups, 24, elems), f32),
            pltpu.VMEM((rows, cdev), f32),
            pltpu.VMEM((nsub, 3, elems), f32),
            dma((3,)), dma((5,)),
            dma((n - 1,)), dma((n - 1,)),
            dma((bits,)), dma((bits,)),
            dma((groups * (n - 1),)), dma((groups * (n - 1),)),
            dma((nsub - 1,)), dma((nsub - 1,)),
            dma((cdev // chunk,)),
        ],
        compiler_params=pltpu.CompilerParams(
            collective_id=0, has_side_effects=True, vmem_limit_bytes=64 * 2**20
        ),
        name="atlas",
    )(tverts, ttris, local, partner.T, controls, by_axis(momenta), by_axis(tv), by_axis(tt))
    template_grad, grads = pl.pallas_call(
        deliver,
        out_shape=(
            jax.ShapeDtypeStruct((3, elems), f32),
            jax.ShapeDtypeStruct((3, subjects, cdev), f32),
        ),
        in_specs=[hbm, hbm],
        out_specs=(hbm, hbm),
        scratch_shapes=[
            pltpu.VMEM((3, elems), f32), pltpu.VMEM((3, subjects, cdev), f32), dma((4,)), dma((4,)),
        ],
        name="deliver",
    )(template_grad, grads.reshape(3, subjects, cdev))
    return template_grad, grads.transpose(1, 0, 2)


def solution(mesh):
    return jax.shard_map(
        functools.partial(on_device, mesh.shape["blk"], mesh.shape["subj"]),
        mesh=mesh,
        in_specs=(
            P(None, ("groups", "blk")),
            P(None, ("groups", "blk")),
            P("blk", None),
            P(None, "blk"),
            P(),
            P(("groups", "subj"), None, None),
            P(("groups", "subj"), None, "blk"),
            P(("groups", "subj"), None, "blk"),
        ),
        out_specs=(P(None, ("groups", "blk")), P(("groups", "subj"), None, "blk")),
        check_vma=False,
    )
```

```python
import functools
import math

import jax
import jax.numpy as jnp
from jax import lax
from jax.experimental import pallas as pl
from jax.experimental.pallas import tpu as pltpu
from jax.sharding import PartitionSpec as P

AREA_SQ = 0.25
SCALE = math.sqrt(math.log2(math.e))
LANES = 128
ROWS = 16
MESH = pl.DeviceIdType.MESH
f32, bf16 = jnp.float32, jnp.bfloat16
NT = (((1,), (1,)), ((), ()))
NN = (((1,), (0,)), ((), ()))


def split(value):
    high = value.astype(bf16)
    return high, (value - high.astype(f32)).astype(bf16)


def mxu(a, b, dims):
    return lax.dot_general(a, b, dims, preferred_element_type=f32)


def pick_lanes(halves, indices):
    out = []
    for idx in indices:
        low = idx & (LANES - 1)
        value = jnp.take_along_axis(halves[0], low, axis=1, mode="promise_in_bounds")
        for h in range(1, len(halves)):
            other = jnp.take_along_axis(halves[h], low, axis=1, mode="promise_in_bounds")
            value = jnp.where(idx >= h * LANES, other, value)
        out.append(value)
    return out


def cross(a, b):
    return [
        a[1] * b[2] - a[2] * b[1],
        a[2] * b[0] - a[0] * b[2],
        a[0] * b[1] - a[1] * b[0],
    ]


def edges(verts, corner_ids):
    corners = [[pick_lanes(verts[d], corner_ids[k]) for d in range(3)] for k in range(3)]
    pieces = []
    for h in range(len(corner_ids[0])):
        a, b, c = [[corners[k][d][h] for d in range(3)] for k in range(3)]
        center = [(a[d] + b[d] + c[d]) * (1.0 / 3.0) for d in range(3)]
        one = [b[d] - a[d] for d in range(3)]
        two = [c[d] - a[d] for d in range(3)]
        normal = [0.5 * v for v in cross(one, two)]
        pieces.append((center, one, two, normal))
    return pieces


def root_norm(normal):
    return jnp.sqrt(normal[0] * normal[0] + normal[1] * normal[1] + normal[2] * normal[2] + AREA_SQ)


def kernel(
    cfg,
    x_hbm, tris_hbm, local_hbm, partner_hbm, ctrl_hbm, mom_hbm, tv_hbm, tt_hbm,
    tg_out, mg_hbm,
    x_ref, tris_ref, local_ref, partner_ref, ctrl_ref, mom, tv, tt, xs, xl, csc, khi, klo, khi_b, klo_b, bhi, blo, vel, own, tgt, mates, stk, uw, pb, inn, t_hi, t_lo, gout, geo, hot, cots, mg, tgs,
    mom_sem, t_sem, xs_s, xs_r, pn_s, pn_r, ct_s, ct_r, tg_s, tg_r, out_sem,
):
    n, nsub, subjects, elems, ctrl, cdev, bits, chunk = cfg
    rows = 3 * subjects
    halves = elems // LANES
    groups = subjects // 8
    me = lax.axis_index("blk")
    sub = lax.axis_index("subj")

    loads = [
        pltpu.make_async_copy(x_hbm, x_ref, mom_sem.at[0]),
        pltpu.make_async_copy(ctrl_hbm, ctrl_ref, mom_sem.at[1]),
        pltpu.make_async_copy(mom_hbm, mom, mom_sem.at[2]),
    ]
    tloads = [
        pltpu.make_async_copy(tris_hbm, tris_ref, t_sem.at[0]),
        pltpu.make_async_copy(tv_hbm, tv, t_sem.at[1]),
        pltpu.make_async_copy(tt_hbm, tt, t_sem.at[2]),
        pltpu.make_async_copy(local_hbm, local_ref, t_sem.at[3]),
        pltpu.make_async_copy(partner_hbm, partner_ref, t_sem.at[4]),
    ]
    for c in loads + tloads:
        c.start()

    def over_rows(value):
        return jnp.sum(value, axis=0, keepdims=True)

    barrier = pltpu.get_barrier_semaphore()
    for o in range(1, n):
        pl.semaphore_signal(barrier, inc=1, device_id={"blk": me ^ o}, device_id_type=MESH)
    for o in range(1, nsub):
        pl.semaphore_signal(
            barrier, inc=1, device_id={"subj": lax.rem(sub + o, nsub)}, device_id_type=MESH
        )

    def augment(points, near, factor):
        scaled = points * SCALE
        square = over_rows(scaled * scaled)
        ones = jnp.full_like(square, near)
        pair = [ones, square * near] if near < 0 else [square, ones]
        rest = jnp.zeros((3, points.shape[1]), f32)
        return jnp.concatenate([scaled * factor] + pair + [rest], axis=0)

    def thirds(value):
        one = value.astype(bf16).astype(f32)
        two = (value - one).astype(bf16).astype(f32)
        return one, two, value - one - two

    def spread(points, slot):
        b1, b2, b3 = thirds(augment(points, -1.0, 2.0))
        xl[slot] = jnp.concatenate([b1, b1, b2, b2, b1, b3], axis=0).T.astype(bf16)

    loads[0].wait()
    spread(x_ref[...], 0)
    loads[1].wait()
    for i in range(0, ctrl, 1024):
        here = slice(i, i + 1024)
        a1, a2, a3 = thirds(augment(ctrl_ref[:, here], 1.0, 1.0))
        csc[:, here] = jnp.concatenate([a1, a2, a1, a2, a3, a1], axis=0).astype(bf16)
    vel[...] = jnp.zeros_like(vel)

    def kernel_chunk(slot, start, hi_to, lo_to):
        power = mxu(xl[slot], csc[:, pl.ds(start, chunk)], NN)
        hi, lo = split(jnp.exp2(power))
        hi_to[...] = hi
        lo_to[...] = lo

    loads[2].wait()

    def weigh(start, hi_from, lo_from):
        m = mom[:, pl.ds(start, chunk)]
        weighted = [m]
        for d in range(3):
            weighted.append(m * ctrl_ref[d : d + 1, pl.ds(start, chunk)])
        pairs = [split(w) for w in weighted]
        hi = jnp.concatenate([p[0] for p in pairs], axis=0)
        both = mxu(jnp.concatenate([hi] + [p[1] for p in pairs], axis=0), hi_from[...], NT)
        vel[...] += both[0 : 4 * rows] + both[4 * rows :] + mxu(hi, lo_from[...], NT)

    own_chunks = cdev // chunk
    main = ctrl // chunk - own_chunks
    span = lambda c: slice(c * chunk, (c + 1) * chunk)

    def where(j):
        return pl.multiple_of(lax.rem((me + 1) * cdev + j * chunk, ctrl), chunk)

    now, later = (khi, klo), (khi_b, klo_b)
    kernel_chunk(0, where(0), *now)
    odd = main % 2
    if odd:
        kernel_chunk(0, where(1), *later)
        weigh(where(0), *now)
        now, later = later, now

    def forward(i, carry):
        j = odd + 2 * i
        kernel_chunk(0, where(j + 1), *later)
        weigh(where(j), *now)
        kernel_chunk(0, where(j + 2), *now)
        weigh(where(j + 1), *later)
        return carry

    lax.fori_loop(0, main // 2, forward, 0)
    bhi[0, :, span(0)] = now[0][...]
    blo[0, :, span(0)] = now[1][...]
    for c in range(own_chunks):
        if c + 1 < own_chunks:
            kernel_chunk(0, where(main + c + 1), bhi.at[0, :, span(c + 1)], blo.at[0, :, span(c + 1)])
        weigh(where(main + c), *(now if c == 0 else (bhi.at[0, :, span(c)], blo.at[0, :, span(c)])))

    pl.semaphore_wait(barrier, n - 1 + nsub - 1)

    def to_blk(src, dst, ssem, rsem, o, s):
        return pltpu.make_async_remote_copy(
            src_ref=src, dst_ref=dst, send_sem=ssem.at[s], recv_sem=rsem.at[s],
            device_id={"blk": me ^ o}, device_id_type=MESH,
        )

    x_sends = [to_blk(x_ref, xs.at[o - 1], xs_s, xs_r, o, o - 1) for o in range(1, n)]
    for c in x_sends:
        c.start()

    tloads[0].wait()
    lane = lambda h: slice(h * LANES, (h + 1) * LANES)
    for g in range(groups):
        verts = [
            [
                x_ref[d : d + 1, lane(h)] + vel[pl.ds(d * subjects + g * 8, 8), lane(h)]
                for h in range(halves)
            ]
            for d in range(3)
        ]
        ids = [
            [jnp.broadcast_to(tris_ref[k : k + 1, lane(h)], (8, LANES)) for h in range(halves)]
            for k in range(3)
        ]
        for h, (center, one, two, normal) in enumerate(edges(verts, ids)):
            nu = root_norm(normal)
            inv = 1.0 / jnp.sqrt(nu)
            for d in range(3):
                own[d, g, h] = center[d] * SCALE
                own[3 + d, g, h] = normal[d] * inv
                geo[d, g, h] = one[d]
                geo[3 + d, g, h] = two[d]
                geo[6 + d, g, h] = normal[d]
            geo[9, g, h] = nu

    p_sends = [to_blk(own, mates.at[b], pn_s, pn_r, 2**b, b) for b in range(bits)]
    for c in p_sends:
        c.start()

    for c in tloads[1:]:
        c.wait()
    for g in range(groups):
        part = lambda d: pl.ds(d * subjects + g * 8, 8)
        verts = [[tv[part(d), lane(h)] for h in range(halves)] for d in range(3)]
        ids = [[tt[part(k), lane(h)] for h in range(halves)] for k in range(3)]
        for h, (center, one, two, normal) in enumerate(edges(verts, ids)):
            inv = 1.0 / jnp.sqrt(root_norm(normal))
            for d in range(3):
                tgt[d, g, h] = center[d] * SCALE
                tgt[3 + d, g, h] = normal[d] * inv

    for k in range(3):
        vertex = lax.broadcasted_iota(jnp.int32, (elems, elems), 0)
        hot[:, k * elems : (k + 1) * elems] = jnp.where(
            vertex == tris_ref[k : k + 1, :], 1.0, 0.0
        ).astype(bf16)

    every = list(range(halves))
    as_float = lambda v: v.astype(f32)

    def stack(src, q, w, g, h):
        products = [w[d] * q[k] for d in range(3) for k in range(3)]
        for r, value in enumerate(w + products + q + [jnp.zeros_like(q[0])]):
            stk[src, h, pl.ds(g * 8 * ROWS + r, 8, stride=ROWS), :] = value

    for g in range(groups):
        for h in every:
            stack(0, [own[d, g, h] for d in range(3)], [own[3 + d, g, h] for d in range(3)], g, h)
            stack(1, [tgt[d, g, h] for d in range(3)], [tgt[3 + d, g, h] for d in range(3)], g, h)

    wide = lambda parts: jnp.concatenate(parts, axis=1) if len(parts) > 1 else parts[0]
    first = lambda s: s * ROWS if isinstance(s, int) else pl.multiple_of(s * ROWS, ROWS)
    width_of = lambda blocks: slice(0, len(blocks) * LANES)

    def rows_of(s, src, blocks):
        return [stk[src, b, pl.ds(first(s), ROWS), :] for b in blocks]

    def multiply(s, slot, item):
        src, tasks = item
        for own_rows, blocks, _ in tasks:
            hi, lo = split(wide(rows_of(s, src, blocks)))
            inn[slot, own_rows, width_of(blocks)] = mxu(
                uw[s, own_rows, :], jnp.concatenate([hi, lo, hi, lo], axis=0), NN
            )

    def weigh_pairs(s, slot, item):
        src, tasks = item
        for own_rows, blocks, _ in tasks:
            for r in range(own_rows.start, own_rows.stop, 32):
                here = slice(r, r + 32)
                total = None
                for d in range(3):
                    q = wide([stk[src, b, pl.ds(first(s) + 12 + d, 1), :] for b in blocks])
                    off = wide([pb[s, d, here, :]] * len(blocks)) - q
                    total = off * off if total is None else total + off * off
                t = jnp.exp2(-total) * inn[slot, here, width_of(blocks)]
                hi, lo = split(t)
                t_hi[slot, here, width_of(blocks)] = hi
                t_lo[slot, here, width_of(blocks)] = lo

    def collect(s, slot, item, to, fresh):
        src, tasks = item
        for own_rows, blocks, coefs in tasks:
            parts = rows_of(s, src, blocks)
            for a in every:
                if not own_rows.start <= a * LANES < own_rows.stop:
                    continue
                hi, lo = split(wide([part * c for part, c in zip(parts, coefs[a])]))
                both = mxu(
                    jnp.concatenate([hi, lo], axis=0), t_hi[slot, lane(a), width_of(blocks)], NT
                )
                term = both[0:ROWS] + both[ROWS:]
                term = term + mxu(hi, t_lo[slot, lane(a), width_of(blocks)], NT)
                here = pl.ds(first(s), ROWS)
                gout[to, a, here, :] = term if fresh else gout[to, a, here, :] + term

    def sweep(items, to, start, stop, ahead=None):
        last = stop - 1
        many = len(items)
        per = 1 if many % 2 == 0 else 2
        steps = [(ds, x) for ds in range(per) for x in range(many)]

        def body(i, carry):
            s = start + per * i
            before = (jnp.maximum(s - 1, start), many - 1)
            for at_step, (ds, x) in enumerate(steps):
                slot = at_step % 2
                here = s + ds
                collect(before[0], 1 - slot, items[before[1]], to, before[1] == 0)
                weigh_pairs(here, slot, items[x])
                if at_step + 1 < len(steps):
                    more, y = steps[at_step + 1]
                    multiply(s + more, 1 - slot, items[y])
                else:
                    multiply(jnp.minimum(s + per, last), 1 - slot, items[0])
                before = (here, x)
            if ahead is not None:
                for ds in range(per):
                    ahead(jnp.minimum(s + per + 1 + ds, last))
            return carry

        if ahead is not None:
            for s in range(per + 1):
                ahead(start + s)
        multiply(start, 0, items[0])
        lax.fori_loop(0, (stop - start) // per, body, 0)
        collect(last, 1, items[-1], to, many == 1)

    def prepare(s):
        row = lax.broadcasted_iota(jnp.int32, (ROWS, LANES), 0)
        for a in every:
            mine = stk[0, a, pl.ds(first(s), ROWS), :]
            weights = jnp.where(row < 3, mine, 0.0)
            hi = weights.astype(bf16).astype(f32)
            lo = weights - hi
            columns = jnp.concatenate([hi, hi, lo, lo, mine], axis=0).T
            uw[s, lane(a), :] = columns[:, 0 : 4 * ROWS].astype(bf16)
            for d in range(3):
                at_d = 4 * ROWS + 12 + d
                pb[s, d, lane(a), :] = jnp.broadcast_to(columns[:, at_d : at_d + 1], (LANES, LANES))

    whole = slice(0, elems)
    local = {a: [as_float(local_ref[a, b] + local_ref[b, a]) for b in every] for a in every}
    near = [(0, [(whole, every, local)])]
    near.append((1, [(lane(a), [a], {a: [-2.0]}) for a in every]))
    sweep(near, 0, 0, subjects, prepare)

    distant = []
    for bit in range(bits):
        p_sends[bit].wait_recv()
        for g in range(groups):
            for h in every:
                take = lambda d: mates[bit, d, g, h]
                stack(2 + bit, [take(d) for d in range(3)], [take(3 + d) for d in range(3)], g, h)
        coefs = {a: [] for a in every}
        for a in every:
            for b in every:
                count = jnp.int32(0)
                for r in range(4):
                    if r % (n.bit_length() - 1) == bit:
                        count = count + jnp.where(partner_ref[a, r] == b, 2, 0)
                coefs[a].append(as_float(count))
        distant.append((2 + bit, [(whole, every, coefs)]))

    width = 1.0 / LANES
    pack = 3 * 8

    def halve(value):
        hi = value.astype(bf16).astype(f32)
        return jnp.concatenate([hi, value - hi], axis=0).astype(bf16)

    def finish(g):
        corner = [[[None] * halves for _ in range(3)] for _ in range(3)]
        for h in range(halves):
            one = [geo[d, g, h] for d in range(3)]
            two = [geo[3 + d, g, h] for d in range(3)]
            u = [geo[6 + d, g, h] for d in range(3)]
            inv = 1.0 / geo[9, g, h]
            root = jnp.sqrt(geo[9, g, h])
            part = lambda i, r: gout[i, h, pl.ds(g * 8 * ROWS + r, 8, stride=ROWS), :]
            take = lambda r: part(0, r) + part(1, r)
            turned = [root * take(d) for d in range(3)]
            total = u[0] * turned[0] + u[1] * turned[1] + u[2] * turned[2]
            moved = []
            for k in range(3):
                mixed = [u[d] * take(3 + 3 * d + k) for d in range(3)]
                moved.append(own[k, g, h] * total - root * (mixed[0] + mixed[1] + mixed[2]))
            shrink = inv * inv * inv * total
            gp = [moved[d] * inv * (-2.0 * width / SCALE / 3.0) for d in range(3)]
            gu = [(2.0 * inv * turned[d] - u[d] * shrink) * (0.5 * width) for d in range(3)]
            g_one = cross(two, gu)
            g_two = cross(gu, one)
            for d in range(3):
                corner[0][d][h] = gp[d] - g_one[d] - g_two[d]
                corner[1][d][h] = gp[d] + g_one[d]
                corner[2][d][h] = gp[d] + g_two[d]
        value = jnp.concatenate(
            [
                jnp.concatenate([corner[k][d][h] for d in range(3)], axis=0)
                for k in range(3)
                for h in range(halves)
            ],
            axis=1,
        )
        both = mxu(halve(value), hot[...], NT)
        cots[0, g] = both[0:pack] + both[pack:]

    c_sends = []
    for g in range(groups):
        sweep(distant, 1, g * 8, g * 8 + 8)
        finish(g)
        for o in range(1, n):
            at_g = g * (n - 1) + o - 1
            c_sends.append(to_blk(cots.at[0, g], cots.at[o, g], ct_s, ct_r, o, at_g))
            c_sends[-1].start()

    def vel_of(c, g):
        base = c * rows + g * 8
        return jnp.concatenate([vel[pl.ds(base + d * subjects, 8), :] for d in range(3)], axis=0)

    factor = 1.0 / (subjects * nsub)
    over_groups = lambda f: sum(over_rows(f(g, cots[0, g])) for g in range(groups))
    plain = over_groups(lambda g, cot: cot * vel_of(0, g))
    for d in range(3):
        direct = over_groups(lambda g, cot: cot[d * 8 : (d + 1) * 8])
        moved = over_groups(lambda g, cot: cot * vel_of(d + 1, g))
        tgs[sub, pl.ds(d, 1), :] = factor * (direct - 2.0 * (x_ref[d : d + 1, :] * plain - moved))

    g_sends = []
    for o in range(1, nsub):
        g_sends.append(
            pltpu.make_async_remote_copy(
                src_ref=tgs.at[sub], dst_ref=tgs.at[sub], send_sem=tg_s.at[o - 1],
                recv_sem=tg_r.at[o - 1], device_id={"subj": lax.rem(sub + o, nsub)},
                device_id_type=MESH,
            )
        )
    for c in g_sends:
        c.start()

    for o in range(1, n):
        x_sends[o - 1].wait_recv()
        spread(xs[o - 1], o)

    for o in range(1, n):
        for c in range(own_chunks):
            start = pl.multiple_of(me * cdev + c * chunk, chunk)
            kernel_chunk(o, start, bhi.at[o, :, span(c)], blo.at[o, :, span(c)])

    outs = []

    def backward(o):
        halves_of = [cots[o, g] for g in range(groups)]
        value = jnp.concatenate(halves_of, axis=0)
        high = value.astype(bf16).astype(f32)
        two = jnp.concatenate([high, value - high], axis=0).astype(bf16)
        high = high.astype(bf16)

        for c in range(own_chunks):
            both = mxu(two, bhi[o, :, span(c)], NN)
            term = both[0:rows] + both[rows:] + mxu(high, blo[o, :, span(c)], NN)
            for g in range(groups):
                for d in range(3):
                    base = g * pack + d * 8
                    piece = term[base : base + 8]
                    block = pl.ds(d * subjects + g * 8, 8)
                    mg[block, span(c)] = mg[block, span(c)] + piece if o else piece
            if o == n - 1:
                outs.append(
                    pltpu.make_async_copy(mg.at[:, span(c)], mg_hbm.at[:, span(c)], out_sem.at[c])
                )
                outs[-1].start()

    backward(0)
    for o in range(1, n):
        for g in range(groups):
            c_sends[g * (n - 1) + o - 1].wait_recv()
        backward(o)

    for c in g_sends:
        c.wait_recv()
    tg_sum = tgs[0]
    for o in range(1, nsub):
        tg_sum = tg_sum + tgs[o]
    tg_out[...] = tg_sum
    for c in x_sends + p_sends + c_sends + g_sends:
        c.wait_send()
    for c in outs:
        c.wait()


def deliver(tg, mg, tg_out, mg_out, tg_held, held, sem_in, sem_out):
    moves = []
    for d in range(3):
        moves.append(
            (
                pltpu.make_async_copy(mg.at[d], held.at[d], sem_in.at[d]),
                pltpu.make_async_copy(held.at[d], mg_out.at[d], sem_out.at[d]),
            )
        )
    moves.append(
        (
            pltpu.make_async_copy(tg, tg_held, sem_in.at[3]),
            pltpu.make_async_copy(tg_held, tg_out, sem_out.at[3]),
        )
    )
    for c in moves:
        c[0].start()
    for c in moves:
        c[0].wait()
        c[1].start()
    for c in moves:
        c[1].wait()


def on_device(n, nsub, tverts, ttris, local, partner, controls, momenta, tv, tt):
    subjects, _, ctrl = momenta.shape
    elems = tverts.shape[1]
    halves = elems // LANES
    groups = subjects // 8
    rows = 3 * subjects
    cdev = ctrl // n
    bits = min(4, n.bit_length() - 1)
    chunk = min(512, cdev)
    cfg = (n, nsub, subjects, elems, ctrl, cdev, bits, chunk)
    vmem = pl.BlockSpec(memory_space=pltpu.VMEM)
    hbm = pl.BlockSpec(memory_space=pltpu.HBM)
    panel = (6, groups, halves, 8, LANES)
    dma = pltpu.SemaphoreType.DMA
    by_axis = lambda v: v.transpose(1, 0, 2).reshape(rows, v.shape[2])
    template_grad, grads = pl.pallas_call(
        functools.partial(kernel, cfg),
        out_shape=(
            jax.ShapeDtypeStruct((3, elems), f32),
            jax.ShapeDtypeStruct((rows, cdev), f32),
        ),
        in_specs=[hbm] * 8,
        out_specs=(vmem, hbm),
        scratch_shapes=[
            pltpu.VMEM((3, elems), f32),
            pltpu.VMEM((3, elems), jnp.int32),
            pltpu.SMEM(local.shape, jnp.int32),
            pltpu.SMEM(partner.shape[::-1], jnp.int32),
            pltpu.VMEM((3, ctrl), f32),
            pltpu.VMEM((rows, ctrl), f32),
            pltpu.VMEM((rows, elems), f32),
            pltpu.VMEM((rows, elems), jnp.int32),
            pltpu.VMEM((n - 1, 3, elems), f32),
            pltpu.VMEM((n, elems, 48), bf16),
            pltpu.VMEM((48, ctrl), bf16),
            pltpu.VMEM((elems, chunk), bf16),
            pltpu.VMEM((elems, chunk), bf16),
            pltpu.VMEM((elems, chunk), bf16),
            pltpu.VMEM((elems, chunk), bf16),
            pltpu.VMEM((n, elems, cdev), bf16),
            pltpu.VMEM((n, elems, cdev), bf16),
            pltpu.VMEM((4 * rows, elems), f32),
            pltpu.VMEM(panel, f32),
            pltpu.VMEM(panel, f32),
            pltpu.VMEM((bits,) + panel, f32),
            pltpu.VMEM((2 + bits, halves, subjects * ROWS, LANES), f32),
            pltpu.VMEM((subjects, elems, 4 * ROWS), bf16),
            pltpu.VMEM((subjects, 3, elems, LANES), f32),
            pltpu.VMEM((2, elems, elems), f32),
            pltpu.VMEM((2, elems, elems), bf16),
            pltpu.VMEM((2, elems, elems), bf16),
            pltpu.VMEM((2, halves, subjects * ROWS, LANES), f32),
            pltpu.VMEM((10,) + panel[1:], f32),
            pltpu.VMEM((elems, 3 * elems), bf16),
            pltpu.VMEM((n, groups, 24, elems), f32),
            pltpu.VMEM((rows, cdev), f32),
            pltpu.VMEM((nsub, 3, elems), f32),
            dma((3,)), dma((5,)),
            dma((n - 1,)), dma((n - 1,)),
            dma((bits,)), dma((bits,)),
            dma((groups * (n - 1),)), dma((groups * (n - 1),)),
            dma((nsub - 1,)), dma((nsub - 1,)),
            dma((cdev // chunk,)),
        ],
        compiler_params=pltpu.CompilerParams(
            collective_id=0, has_side_effects=True, vmem_limit_bytes=64 * 2**20
        ),
        name="atlas",
    )(tverts, ttris, local, partner.T, controls, by_axis(momenta), by_axis(tv), by_axis(tt))
    template_grad, grads = pl.pallas_call(
        deliver,
        out_shape=(
            jax.ShapeDtypeStruct((3, elems), f32),
            jax.ShapeDtypeStruct((3, subjects, cdev), f32),
        ),
        in_specs=[hbm, hbm],
        out_specs=(hbm, hbm),
        scratch_shapes=[
            pltpu.VMEM((3, elems), f32), pltpu.VMEM((3, subjects, cdev), f32), dma((4,)), dma((4,)),
        ],
        name="deliver",
    )(template_grad, grads.reshape(3, subjects, cdev))
    return template_grad, grads.transpose(1, 0, 2)


def solution(mesh):
    return jax.shard_map(
        functools.partial(on_device, mesh.shape["blk"], mesh.shape["subj"]),
        mesh=mesh,
        in_specs=(
            P(None, ("groups", "blk")),
            P(None, ("groups", "blk")),
            P("blk", None),
            P(None, "blk"),
            P(),
            P(("groups", "subj"), None, None),
            P(("groups", "subj"), None, "blk"),
            P(("groups", "subj"), None, "blk"),
        ),
        out_specs=(P(None, ("groups", "blk")), P(("groups", "subj"), None, "blk")),
        check_vma=False,
    )
```

```python
import functools
import math

import jax
import jax.numpy as jnp
from jax import lax
from jax.experimental import pallas as pl
from jax.experimental.pallas import tpu as pltpu
from jax.sharding import PartitionSpec as P

AREA_SQ = 0.25
SCALE = math.sqrt(math.log2(math.e))
LANES = 128
ROWS = 16
MESH = pl.DeviceIdType.MESH
f32, bf16 = jnp.float32, jnp.bfloat16
NT = (((1,), (1,)), ((), ()))
NN = (((1,), (0,)), ((), ()))


def split(value):
    high = value.astype(bf16)
    return high, (value - high.astype(f32)).astype(bf16)


def mxu(a, b, dims):
    return lax.dot_general(a, b, dims, preferred_element_type=f32)


def pick_lanes(halves, indices):
    out = []
    for idx in indices:
        low = idx & (LANES - 1)
        value = jnp.take_along_axis(halves[0], low, axis=1, mode="promise_in_bounds")
        for h in range(1, len(halves)):
            other = jnp.take_along_axis(halves[h], low, axis=1, mode="promise_in_bounds")
            value = jnp.where(idx >= h * LANES, other, value)
        out.append(value)
    return out


def cross(a, b):
    return [
        a[1] * b[2] - a[2] * b[1],
        a[2] * b[0] - a[0] * b[2],
        a[0] * b[1] - a[1] * b[0],
    ]


def edges(verts, corner_ids):
    corners = [[pick_lanes(verts[d], corner_ids[k]) for d in range(3)] for k in range(3)]
    pieces = []
    for h in range(len(corner_ids[0])):
        a, b, c = [[corners[k][d][h] for d in range(3)] for k in range(3)]
        center = [(a[d] + b[d] + c[d]) * (1.0 / 3.0) for d in range(3)]
        one = [b[d] - a[d] for d in range(3)]
        two = [c[d] - a[d] for d in range(3)]
        normal = [0.5 * v for v in cross(one, two)]
        pieces.append((center, one, two, normal))
    return pieces


def root_norm(normal):
    return jnp.sqrt(normal[0] * normal[0] + normal[1] * normal[1] + normal[2] * normal[2] + AREA_SQ)


def kernel(
    cfg,
    x_hbm, tris_hbm, local_hbm, partner_hbm, ctrl_hbm, mom_hbm, tv_hbm, tt_hbm,
    tg_out, mg_hbm,
    x_ref, tris_ref, local_ref, partner_ref, ctrl_ref, mom, tv, tt, xs, xl, csc, khi, klo, khi_b, klo_b, bhi, blo, vel, own, tgt, mates, stk, uw, pb, inn, t_hi, t_lo, gout, geo, hot, cots, mg, tgs,
    mom_sem, t_sem, xs_s, xs_r, pn_s, pn_r, ct_s, ct_r, tg_s, tg_r, out_sem,
):
    n, nsub, subjects, elems, ctrl, cdev, bits, chunk = cfg
    rows = 3 * subjects
    halves = elems // LANES
    groups = subjects // 8
    me = lax.axis_index("blk")
    sub = lax.axis_index("subj")

    loads = [
        pltpu.make_async_copy(x_hbm, x_ref, mom_sem.at[0]),
        pltpu.make_async_copy(ctrl_hbm, ctrl_ref, mom_sem.at[1]),
        pltpu.make_async_copy(mom_hbm, mom, mom_sem.at[2]),
    ]
    tloads = [
        pltpu.make_async_copy(tris_hbm, tris_ref, t_sem.at[0]),
        pltpu.make_async_copy(tv_hbm, tv, t_sem.at[1]),
        pltpu.make_async_copy(tt_hbm, tt, t_sem.at[2]),
        pltpu.make_async_copy(local_hbm, local_ref, t_sem.at[3]),
        pltpu.make_async_copy(partner_hbm, partner_ref, t_sem.at[4]),
    ]
    for c in loads + tloads:
        c.start()

    def over_rows(value):
        return jnp.sum(value, axis=0, keepdims=True)

    barrier = pltpu.get_barrier_semaphore()
    for o in range(1, n):
        pl.semaphore_signal(barrier, inc=1, device_id={"blk": me ^ o}, device_id_type=MESH)
    for o in range(1, nsub):
        pl.semaphore_signal(
            barrier, inc=1, device_id={"subj": lax.rem(sub + o, nsub)}, device_id_type=MESH
        )

    def augment(points, near, factor):
        scaled = points * SCALE
        square = over_rows(scaled * scaled)
        ones = jnp.full_like(square, near)
        pair = [ones, square * near] if near < 0 else [square, ones]
        rest = jnp.zeros((3, points.shape[1]), f32)
        return jnp.concatenate([scaled * factor] + pair + [rest], axis=0)

    def thirds(value):
        one = value.astype(bf16).astype(f32)
        two = (value - one).astype(bf16).astype(f32)
        return one, two, value - one - two

    def spread(points, slot):
        b1, b2, b3 = thirds(augment(points, -1.0, 2.0))
        xl[slot] = jnp.concatenate([b1, b1, b2, b2, b1, b3], axis=0).T.astype(bf16)

    loads[0].wait()
    spread(x_ref[...], 0)
    loads[1].wait()
    for i in range(0, ctrl, 1024):
        here = slice(i, i + 1024)
        a1, a2, a3 = thirds(augment(ctrl_ref[:, here], 1.0, 1.0))
        csc[:, here] = jnp.concatenate([a1, a2, a1, a2, a3, a1], axis=0).astype(bf16)
    vel[...] = jnp.zeros_like(vel)

    def kernel_chunk(slot, start, hi_to, lo_to):
        power = mxu(xl[slot], csc[:, pl.ds(start, chunk)], NN)
        hi, lo = split(jnp.exp2(power))
        hi_to[...] = hi
        lo_to[...] = lo

    loads[2].wait()

    def weigh(start, hi_from, lo_from):
        m = mom[:, pl.ds(start, chunk)]
        weighted = [m]
        for d in range(3):
            weighted.append(m * ctrl_ref[d : d + 1, pl.ds(start, chunk)])
        pairs = [split(w) for w in weighted]
        hi = jnp.concatenate([p[0] for p in pairs], axis=0)
        both = mxu(jnp.concatenate([hi] + [p[1] for p in pairs], axis=0), hi_from[...], NT)
        vel[...] += both[0 : 4 * rows] + both[4 * rows :] + mxu(hi, lo_from[...], NT)

    own_chunks = cdev // chunk
    main = ctrl // chunk - own_chunks
    span = lambda c: slice(c * chunk, (c + 1) * chunk)

    def where(j):
        return pl.multiple_of(lax.rem((me + 1) * cdev + j * chunk, ctrl), chunk)

    now, later = (khi, klo), (khi_b, klo_b)
    kernel_chunk(0, where(0), *now)
    odd = main % 2
    if odd:
        kernel_chunk(0, where(1), *later)
        weigh(where(0), *now)
        now, later = later, now

    def forward(i, carry):
        j = odd + 2 * i
        kernel_chunk(0, where(j + 1), *later)
        weigh(where(j), *now)
        kernel_chunk(0, where(j + 2), *now)
        weigh(where(j + 1), *later)
        return carry

    lax.fori_loop(0, main // 2, forward, 0)
    bhi[0, :, span(0)] = now[0][...]
    blo[0, :, span(0)] = now[1][...]
    for c in range(own_chunks):
        if c + 1 < own_chunks:
            kernel_chunk(0, where(main + c + 1), bhi.at[0, :, span(c + 1)], blo.at[0, :, span(c + 1)])
        weigh(where(main + c), *(now if c == 0 else (bhi.at[0, :, span(c)], blo.at[0, :, span(c)])))

    pl.semaphore_wait(barrier, n - 1 + nsub - 1)

    def to_blk(src, dst, ssem, rsem, o, s):
        return pltpu.make_async_remote_copy(
            src_ref=src, dst_ref=dst, send_sem=ssem.at[s], recv_sem=rsem.at[s],
            device_id={"blk": me ^ o}, device_id_type=MESH,
        )

    x_sends = [to_blk(x_ref, xs.at[o - 1], xs_s, xs_r, o, o - 1) for o in range(1, n)]
    for c in x_sends:
        c.start()

    tloads[0].wait()
    lane = lambda h: slice(h * LANES, (h + 1) * LANES)
    for g in range(groups):
        verts = [
            [
                x_ref[d : d + 1, lane(h)] + vel[pl.ds(d * subjects + g * 8, 8), lane(h)]
                for h in range(halves)
            ]
            for d in range(3)
        ]
        ids = [
            [jnp.broadcast_to(tris_ref[k : k + 1, lane(h)], (8, LANES)) for h in range(halves)]
            for k in range(3)
        ]
        for h, (center, one, two, normal) in enumerate(edges(verts, ids)):
            nu = root_norm(normal)
            inv = 1.0 / jnp.sqrt(nu)
            for d in range(3):
                own[d, g, h] = center[d] * SCALE
                own[3 + d, g, h] = normal[d] * inv
                geo[d, g, h] = one[d]
                geo[3 + d, g, h] = two[d]
                geo[6 + d, g, h] = normal[d]
            geo[9, g, h] = nu

    p_sends = [to_blk(own, mates.at[b], pn_s, pn_r, 2**b, b) for b in range(bits)]
    for c in p_sends:
        c.start()

    for c in tloads[1:]:
        c.wait()
    for g in range(groups):
        part = lambda d: pl.ds(d * subjects + g * 8, 8)
        verts = [[tv[part(d), lane(h)] for h in range(halves)] for d in range(3)]
        ids = [[tt[part(k), lane(h)] for h in range(halves)] for k in range(3)]
        for h, (center, one, two, normal) in enumerate(edges(verts, ids)):
            inv = 1.0 / jnp.sqrt(root_norm(normal))
            for d in range(3):
                tgt[d, g, h] = center[d] * SCALE
                tgt[3 + d, g, h] = normal[d] * inv

    for k in range(3):
        vertex = lax.broadcasted_iota(jnp.int32, (elems, elems), 0)
        hot[:, k * elems : (k + 1) * elems] = jnp.where(
            vertex == tris_ref[k : k + 1, :], 1.0, 0.0
        ).astype(bf16)

    every = list(range(halves))
    as_float = lambda v: v.astype(f32)

    def stack(src, q, w, g, h):
        products = [w[d] * q[k] for d in range(3) for k in range(3)]
        for r, value in enumerate(w + products + q + [jnp.zeros_like(q[0])]):
            stk[src, h, pl.ds(g * 8 * ROWS + r, 8, stride=ROWS), :] = value

    for g in range(groups):
        for h in every:
            stack(0, [own[d, g, h] for d in range(3)], [own[3 + d, g, h] for d in range(3)], g, h)
            stack(1, [tgt[d, g, h] for d in range(3)], [tgt[3 + d, g, h] for d in range(3)], g, h)

    wide = lambda parts: jnp.concatenate(parts, axis=1) if len(parts) > 1 else parts[0]
    first = lambda s: s * ROWS if isinstance(s, int) else pl.multiple_of(s * ROWS, ROWS)
    width_of = lambda blocks: slice(0, len(blocks) * LANES)

    def rows_of(s, src, blocks):
        return [stk[src, b, pl.ds(first(s), ROWS), :] for b in blocks]

    def multiply(s, slot, item):
        src, tasks = item
        for own_rows, blocks, _ in tasks:
            hi, lo = split(wide(rows_of(s, src, blocks)))
            inn[slot, own_rows, width_of(blocks)] = mxu(
                uw[s, own_rows, :], jnp.concatenate([hi, lo, hi, lo], axis=0), NN
            )

    def weigh_pairs(s, slot, item):
        src, tasks = item
        for own_rows, blocks, _ in tasks:
            for r in range(own_rows.start, own_rows.stop, 32):
                here = slice(r, r + 32)
                total = None
                for d in range(3):
                    q = wide([stk[src, b, pl.ds(first(s) + 12 + d, 1), :] for b in blocks])
                    off = wide([pb[s, d, here, :]] * len(blocks)) - q
                    total = off * off if total is None else total + off * off
                t = jnp.exp2(-total) * inn[slot, here, width_of(blocks)]
                hi, lo = split(t)
                t_hi[slot, here, width_of(blocks)] = hi
                t_lo[slot, here, width_of(blocks)] = lo

    def collect(s, slot, item, to, fresh):
        src, tasks = item
        for own_rows, blocks, coefs in tasks:
            parts = rows_of(s, src, blocks)
            for a in every:
                if not own_rows.start <= a * LANES < own_rows.stop:
                    continue
                hi, lo = split(wide([part * c for part, c in zip(parts, coefs[a])]))
                both = mxu(
                    jnp.concatenate([hi, lo], axis=0), t_hi[slot, lane(a), width_of(blocks)], NT
                )
                term = both[0:ROWS] + both[ROWS:]
                term = term + mxu(hi, t_lo[slot, lane(a), width_of(blocks)], NT)
                here = pl.ds(first(s), ROWS)
                gout[to, a, here, :] = term if fresh else gout[to, a, here, :] + term

    def sweep(items, to, start, stop, ahead=None):
        last = stop - 1
        many = len(items)
        per = 1 if many % 2 == 0 else 2
        steps = [(ds, x) for ds in range(per) for x in range(many)]

        def body(i, carry):
            s = start + per * i
            before = (jnp.maximum(s - 1, start), many - 1)
            for at_step, (ds, x) in enumerate(steps):
                slot = at_step % 2
                here = s + ds
                collect(before[0], 1 - slot, items[before[1]], to, before[1] == 0)
                weigh_pairs(here, slot, items[x])
                if at_step + 1 < len(steps):
                    more, y = steps[at_step + 1]
                    multiply(s + more, 1 - slot, items[y])
                else:
                    multiply(jnp.minimum(s + per, last), 1 - slot, items[0])
                before = (here, x)
            if ahead is not None:
                for ds in range(per):
                    ahead(jnp.minimum(s + per + 1 + ds, last))
            return carry

        if ahead is not None:
            for s in range(per + 1):
                ahead(start + s)
        multiply(start, 0, items[0])
        lax.fori_loop(0, (stop - start) // per, body, 0)
        collect(last, 1, items[-1], to, many == 1)

    def prepare(s):
        row = lax.broadcasted_iota(jnp.int32, (ROWS, LANES), 0)
        for a in every:
            mine = stk[0, a, pl.ds(first(s), ROWS), :]
            weights = jnp.where(row < 3, mine, 0.0)
            hi = weights.astype(bf16).astype(f32)
            lo = weights - hi
            columns = jnp.concatenate([hi, hi, lo, lo, mine], axis=0).T
            uw[s, lane(a), :] = columns[:, 0 : 4 * ROWS].astype(bf16)
            for d in range(3):
                at_d = 4 * ROWS + 12 + d
                pb[s, d, lane(a), :] = jnp.broadcast_to(columns[:, at_d : at_d + 1], (LANES, LANES))

    whole = slice(0, elems)
    local = {a: [as_float(local_ref[a, b] + local_ref[b, a]) for b in every] for a in every}
    near = [(0, [(whole, every, local)])]
    near.append((1, [(lane(a), [a], {a: [-2.0]}) for a in every]))
    sweep(near, 0, 0, subjects, prepare)

    distant = []
    for bit in range(bits):
        p_sends[bit].wait_recv()
        for g in range(groups):
            for h in every:
                take = lambda d: mates[bit, d, g, h]
                stack(2 + bit, [take(d) for d in range(3)], [take(3 + d) for d in range(3)], g, h)
        coefs = {a: [] for a in every}
        for a in every:
            for b in every:
                count = jnp.int32(0)
                for r in range(4):
                    if r % (n.bit_length() - 1) == bit:
                        count = count + jnp.where(partner_ref[a, r] == b, 2, 0)
                coefs[a].append(as_float(count))
        distant.append((2 + bit, [(whole, every, coefs)]))

    width = 1.0 / LANES
    pack = 3 * 8

    def halve(value):
        hi = value.astype(bf16).astype(f32)
        return jnp.concatenate([hi, value - hi], axis=0).astype(bf16)

    def finish(g):
        corner = [[[None] * halves for _ in range(3)] for _ in range(3)]
        for h in range(halves):
            one = [geo[d, g, h] for d in range(3)]
            two = [geo[3 + d, g, h] for d in range(3)]
            u = [geo[6 + d, g, h] for d in range(3)]
            inv = 1.0 / geo[9, g, h]
            root = jnp.sqrt(geo[9, g, h])
            part = lambda i, r: gout[i, h, pl.ds(g * 8 * ROWS + r, 8, stride=ROWS), :]
            take = lambda r: part(0, r) + part(1, r)
            turned = [root * take(d) for d in range(3)]
            total = u[0] * turned[0] + u[1] * turned[1] + u[2] * turned[2]
            moved = []
            for k in range(3):
                mixed = [u[d] * take(3 + 3 * d + k) for d in range(3)]
                moved.append(own[k, g, h] * total - root * (mixed[0] + mixed[1] + mixed[2]))
            shrink = inv * inv * inv * total
            gp = [moved[d] * inv * (-2.0 * width / SCALE / 3.0) for d in range(3)]
            gu = [(2.0 * inv * turned[d] - u[d] * shrink) * (0.5 * width) for d in range(3)]
            g_one = cross(two, gu)
            g_two = cross(gu, one)
            for d in range(3):
                corner[0][d][h] = gp[d] - g_one[d] - g_two[d]
                corner[1][d][h] = gp[d] + g_one[d]
                corner[2][d][h] = gp[d] + g_two[d]
        value = jnp.concatenate(
            [
                jnp.concatenate([corner[k][d][h] for d in range(3)], axis=0)
                for k in range(3)
                for h in range(halves)
            ],
            axis=1,
        )
        both = mxu(halve(value), hot[...], NT)
        cots[0, g] = both[0:pack] + both[pack:]

    c_sends = []
    for g in range(groups):
        sweep(distant, 1, g * 8, g * 8 + 8)
        finish(g)
        for o in range(1, n):
            at_g = g * (n - 1) + o - 1
            c_sends.append(to_blk(cots.at[0, g], cots.at[o, g], ct_s, ct_r, o, at_g))
            c_sends[-1].start()

    def vel_of(c, g):
        base = c * rows + g * 8
        return jnp.concatenate([vel[pl.ds(base + d * subjects, 8), :] for d in range(3)], axis=0)

    factor = 1.0 / (subjects * nsub)
    over_groups = lambda f: sum(over_rows(f(g, cots[0, g])) for g in range(groups))
    plain = over_groups(lambda g, cot: cot * vel_of(0, g))
    for d in range(3):
        direct = over_groups(lambda g, cot: cot[d * 8 : (d + 1) * 8])
        moved = over_groups(lambda g, cot: cot * vel_of(d + 1, g))
        tgs[sub, pl.ds(d, 1), :] = factor * (direct - 2.0 * (x_ref[d : d + 1, :] * plain - moved))

    g_sends = []
    for o in range(1, nsub):
        g_sends.append(
            pltpu.make_async_remote_copy(
                src_ref=tgs.at[sub], dst_ref=tgs.at[sub], send_sem=tg_s.at[o - 1],
                recv_sem=tg_r.at[o - 1], device_id={"subj": lax.rem(sub + o, nsub)},
                device_id_type=MESH,
            )
        )
    for c in g_sends:
        c.start()

    for o in range(1, n):
        x_sends[o - 1].wait_recv()
        spread(xs[o - 1], o)

    for o in range(1, n):
        for c in range(own_chunks):
            start = pl.multiple_of(me * cdev + c * chunk, chunk)
            kernel_chunk(o, start, bhi.at[o, :, span(c)], blo.at[o, :, span(c)])

    outs = []

    def backward(o):
        halves_of = [cots[o, g] for g in range(groups)]
        value = jnp.concatenate(halves_of, axis=0)
        high = value.astype(bf16).astype(f32)
        two = jnp.concatenate([high, value - high], axis=0).astype(bf16)
        high = high.astype(bf16)

        for c in range(own_chunks):
            both = mxu(two, bhi[o, :, span(c)], NN)
            term = both[0:rows] + both[rows:] + mxu(high, blo[o, :, span(c)], NN)
            for g in range(groups):
                for d in range(3):
                    base = g * pack + d * 8
                    piece = term[base : base + 8]
                    block = pl.ds(d * subjects + g * 8, 8)
                    mg[block, span(c)] = mg[block, span(c)] + piece if o else piece
            if o == n - 1:
                outs.append(
                    pltpu.make_async_copy(mg.at[:, span(c)], mg_hbm.at[:, span(c)], out_sem.at[c])
                )
                outs[-1].start()

    backward(0)
    for o in range(1, n):
        for g in range(groups):
            c_sends[g * (n - 1) + o - 1].wait_recv()
        backward(o)

    for c in g_sends:
        c.wait_recv()
    tg_sum = tgs[0]
    for o in range(1, nsub):
        tg_sum = tg_sum + tgs[o]
    tg_out[...] = tg_sum
    for c in x_sends + p_sends + c_sends + g_sends:
        c.wait_send()
    for c in outs:
        c.wait()


def deliver(tg, mg, tg_out, mg_out, tg_held, held, sem_in, sem_out):
    moves = []
    for d in range(3):
        moves.append(
            (
                pltpu.make_async_copy(mg.at[d], held.at[d], sem_in.at[d]),
                pltpu.make_async_copy(held.at[d], mg_out.at[d], sem_out.at[d]),
            )
        )
    moves.append(
        (
            pltpu.make_async_copy(tg, tg_held, sem_in.at[3]),
            pltpu.make_async_copy(tg_held, tg_out, sem_out.at[3]),
        )
    )
    for c in moves:
        c[0].start()
    for c in moves:
        c[0].wait()
        c[1].start()
    for c in moves:
        c[1].wait()


def on_device(n, nsub, tverts, ttris, local, partner, controls, momenta, tv, tt):
    subjects, _, ctrl = momenta.shape
    elems = tverts.shape[1]
    halves = elems // LANES
    groups = subjects // 8
    rows = 3 * subjects
    cdev = ctrl // n
    bits = min(4, n.bit_length() - 1)
    chunk = min(1024, cdev)
    cfg = (n, nsub, subjects, elems, ctrl, cdev, bits, chunk)
    vmem = pl.BlockSpec(memory_space=pltpu.VMEM)
    hbm = pl.BlockSpec(memory_space=pltpu.HBM)
    panel = (6, groups, halves, 8, LANES)
    dma = pltpu.SemaphoreType.DMA
    by_axis = lambda v: v.transpose(1, 0, 2).reshape(rows, v.shape[2])
    template_grad, grads = pl.pallas_call(
        functools.partial(kernel, cfg),
        out_shape=(
            jax.ShapeDtypeStruct((3, elems), f32),
            jax.ShapeDtypeStruct((rows, cdev), f32),
        ),
        in_specs=[hbm] * 8,
        out_specs=(vmem, hbm),
        scratch_shapes=[
            pltpu.VMEM((3, elems), f32),
            pltpu.VMEM((3, elems), jnp.int32),
            pltpu.SMEM(local.shape, jnp.int32),
            pltpu.SMEM(partner.shape[::-1], jnp.int32),
            pltpu.VMEM((3, ctrl), f32),
            pltpu.VMEM((rows, ctrl), f32),
            pltpu.VMEM((rows, elems), f32),
            pltpu.VMEM((rows, elems), jnp.int32),
            pltpu.VMEM((n - 1, 3, elems), f32),
            pltpu.VMEM((n, elems, 48), bf16),
            pltpu.VMEM((48, ctrl), bf16),
            pltpu.VMEM((elems, chunk), bf16),
            pltpu.VMEM((elems, chunk), bf16),
            pltpu.VMEM((elems, chunk), bf16),
            pltpu.VMEM((elems, chunk), bf16),
            pltpu.VMEM((n, elems, cdev), bf16),
            pltpu.VMEM((n, elems, cdev), bf16),
            pltpu.VMEM((4 * rows, elems), f32),
            pltpu.VMEM(panel, f32),
            pltpu.VMEM(panel, f32),
            pltpu.VMEM((bits,) + panel, f32),
            pltpu.VMEM((2 + bits, halves, subjects * ROWS, LANES), f32),
            pltpu.VMEM((subjects, elems, 4 * ROWS), bf16),
            pltpu.VMEM((subjects, 3, elems, LANES), f32),
            pltpu.VMEM((2, elems, elems), f32),
            pltpu.VMEM((2, elems, elems), bf16),
            pltpu.VMEM((2, elems, elems), bf16),
            pltpu.VMEM((2, halves, subjects * ROWS, LANES), f32),
            pltpu.VMEM((10,) + panel[1:], f32),
            pltpu.VMEM((elems, 3 * elems), bf16),
            pltpu.VMEM((n, groups, 24, elems), f32),
            pltpu.VMEM((rows, cdev), f32),
            pltpu.VMEM((nsub, 3, elems), f32),
            dma((3,)), dma((5,)),
            dma((n - 1,)), dma((n - 1,)),
            dma((bits,)), dma((bits,)),
            dma((groups * (n - 1),)), dma((groups * (n - 1),)),
            dma((nsub - 1,)), dma((nsub - 1,)),
            dma((cdev // chunk,)),
        ],
        compiler_params=pltpu.CompilerParams(
            collective_id=0, has_side_effects=True, vmem_limit_bytes=64 * 2**20
        ),
        name="atlas",
    )(tverts, ttris, local, partner.T, controls, by_axis(momenta), by_axis(tv), by_axis(tt))
    template_grad, grads = pl.pallas_call(
        deliver,
        out_shape=(
            jax.ShapeDtypeStruct((3, elems), f32),
            jax.ShapeDtypeStruct((3, subjects, cdev), f32),
        ),
        in_specs=[hbm, hbm],
        out_specs=(hbm, hbm),
        scratch_shapes=[
            pltpu.VMEM((3, elems), f32), pltpu.VMEM((3, subjects, cdev), f32), dma((4,)), dma((4,)),
        ],
        name="deliver",
    )(template_grad, grads.reshape(3, subjects, cdev))
    return template_grad, grads.transpose(1, 0, 2)


def solution(mesh):
    return jax.shard_map(
        functools.partial(on_device, mesh.shape["blk"], mesh.shape["subj"]),
        mesh=mesh,
        in_specs=(
            P(None, ("groups", "blk")),
            P(None, ("groups", "blk")),
            P("blk", None),
            P(None, "blk"),
            P(),
            P(("groups", "subj"), None, None),
            P(("groups", "subj"), None, "blk"),
            P(("groups", "subj"), None, "blk"),
        ),
        out_specs=(P(None, ("groups", "blk")), P(("groups", "subj"), None, "blk")),
        check_vma=False,
    )
```

```python
import functools
import math

import jax
import jax.numpy as jnp
from jax import lax
from jax.experimental import pallas as pl
from jax.experimental.pallas import tpu as pltpu
from jax.sharding import PartitionSpec as P

AREA_SQ = 0.25
SCALE = math.sqrt(math.log2(math.e))
LANES = 128
ROWS = 16
MESH = pl.DeviceIdType.MESH
f32, bf16 = jnp.float32, jnp.bfloat16
NT = (((1,), (1,)), ((), ()))
NN = (((1,), (0,)), ((), ()))


def split(value):
    high = value.astype(bf16)
    return high, (value - high.astype(f32)).astype(bf16)


def mxu(a, b, dims):
    return lax.dot_general(a, b, dims, preferred_element_type=f32)


def pick_lanes(halves, indices):
    out = []
    for idx in indices:
        low = idx & (LANES - 1)
        value = jnp.take_along_axis(halves[0], low, axis=1, mode="promise_in_bounds")
        for h in range(1, len(halves)):
            other = jnp.take_along_axis(halves[h], low, axis=1, mode="promise_in_bounds")
            value = jnp.where(idx >= h * LANES, other, value)
        out.append(value)
    return out


def cross(a, b):
    return [
        a[1] * b[2] - a[2] * b[1],
        a[2] * b[0] - a[0] * b[2],
        a[0] * b[1] - a[1] * b[0],
    ]


def edges(verts, corner_ids):
    corners = [[pick_lanes(verts[d], corner_ids[k]) for d in range(3)] for k in range(3)]
    pieces = []
    for h in range(len(corner_ids[0])):
        a, b, c = [[corners[k][d][h] for d in range(3)] for k in range(3)]
        center = [(a[d] + b[d] + c[d]) * (1.0 / 3.0) for d in range(3)]
        one = [b[d] - a[d] for d in range(3)]
        two = [c[d] - a[d] for d in range(3)]
        normal = [0.5 * v for v in cross(one, two)]
        pieces.append((center, one, two, normal))
    return pieces


def root_norm(normal):
    return jnp.sqrt(normal[0] * normal[0] + normal[1] * normal[1] + normal[2] * normal[2] + AREA_SQ)


def kernel(
    cfg,
    x_hbm, tris_hbm, local_hbm, partner_hbm, ctrl_hbm, mom_hbm, tv_hbm, tt_hbm,
    tg_out, mg_hbm,
    x_ref, tris_ref, local_ref, partner_ref, ctrl_ref, mom, tv, tt, xs, xl, csc, khi, klo, khi_b, klo_b, bhi, blo, vel, own, tgt, mates, stk, uw, pb, inn, t_hi, t_lo, gout, geo, hot, cots, mg, tgs,
    mom_sem, t_sem, xs_s, xs_r, pn_s, pn_r, ct_s, ct_r, tg_s, tg_r, out_sem,
):
    n, nsub, subjects, elems, ctrl, cdev, bits, chunk = cfg
    rows = 3 * subjects
    halves = elems // LANES
    groups = subjects // 8
    me = lax.axis_index("blk")
    sub = lax.axis_index("subj")

    loads = [
        pltpu.make_async_copy(x_hbm, x_ref, mom_sem.at[0]),
        pltpu.make_async_copy(ctrl_hbm, ctrl_ref, mom_sem.at[1]),
    ]
    tloads = [
        pltpu.make_async_copy(tris_hbm, tris_ref, t_sem.at[0]),
        pltpu.make_async_copy(tv_hbm, tv, t_sem.at[1]),
        pltpu.make_async_copy(tt_hbm, tt, t_sem.at[2]),
        pltpu.make_async_copy(local_hbm, local_ref, t_sem.at[3]),
        pltpu.make_async_copy(partner_hbm, partner_ref, t_sem.at[4]),
    ]
    def moment_load(j):
        here = pl.ds(pl.multiple_of(lax.rem((me + 1) * cdev + j * chunk, ctrl), chunk), chunk)
        return pltpu.make_async_copy(mom_hbm.at[:, here], mom.at[:, here], mom_sem.at[2 + j])

    for c in loads:
        c.start()
    for j in range(ctrl // chunk):
        moment_load(j).start()
    for c in tloads:
        c.start()

    def over_rows(value):
        return jnp.sum(value, axis=0, keepdims=True)

    barrier = pltpu.get_barrier_semaphore()
    for o in range(1, n):
        pl.semaphore_signal(barrier, inc=1, device_id={"blk": me ^ o}, device_id_type=MESH)
    for o in range(1, nsub):
        pl.semaphore_signal(
            barrier, inc=1, device_id={"subj": lax.rem(sub + o, nsub)}, device_id_type=MESH
        )

    def augment(points, near, factor):
        scaled = points * SCALE
        square = over_rows(scaled * scaled)
        ones = jnp.full_like(square, near)
        pair = [ones, square * near] if near < 0 else [square, ones]
        rest = jnp.zeros((3, points.shape[1]), f32)
        return jnp.concatenate([scaled * factor] + pair + [rest], axis=0)

    def thirds(value):
        one = value.astype(bf16).astype(f32)
        two = (value - one).astype(bf16).astype(f32)
        return one, two, value - one - two

    def spread(points, slot):
        b1, b2, b3 = thirds(augment(points, -1.0, 2.0))
        xl[slot] = jnp.concatenate([b1, b1, b2, b2, b1, b3], axis=0).T.astype(bf16)

    loads[0].wait()
    spread(x_ref[...], 0)
    loads[1].wait()
    for i in range(0, ctrl, 1024):
        here = slice(i, i + 1024)
        a1, a2, a3 = thirds(augment(ctrl_ref[:, here], 1.0, 1.0))
        csc[:, here] = jnp.concatenate([a1, a2, a1, a2, a3, a1], axis=0).astype(bf16)
    vel[...] = jnp.zeros_like(vel)

    def kernel_chunk(slot, start, hi_to, lo_to):
        power = mxu(xl[slot], csc[:, pl.ds(start, chunk)], NN)
        hi, lo = split(jnp.exp2(power))
        hi_to[...] = hi
        lo_to[...] = lo


    def weigh(start, hi_from, lo_from):
        m = mom[:, pl.ds(start, chunk)]
        weighted = [m]
        for d in range(3):
            weighted.append(m * ctrl_ref[d : d + 1, pl.ds(start, chunk)])
        pairs = [split(w) for w in weighted]
        hi = jnp.concatenate([p[0] for p in pairs], axis=0)
        both = mxu(jnp.concatenate([hi] + [p[1] for p in pairs], axis=0), hi_from[...], NT)
        vel[...] += both[0 : 4 * rows] + both[4 * rows :] + mxu(hi, lo_from[...], NT)

    own_chunks = cdev // chunk
    main = ctrl // chunk - own_chunks
    span = lambda c: slice(c * chunk, (c + 1) * chunk)

    def where(j):
        return pl.multiple_of(lax.rem((me + 1) * cdev + j * chunk, ctrl), chunk)

    now, later = (khi, klo), (khi_b, klo_b)
    kernel_chunk(0, where(0), *now)
    odd = main % 2
    if odd:
        moment_load(0).wait()
        kernel_chunk(0, where(1), *later)
        weigh(where(0), *now)
        now, later = later, now

    def forward(i, carry):
        j = odd + 2 * i
        moment_load(j).wait()
        moment_load(j + 1).wait()
        kernel_chunk(0, where(j + 1), *later)
        weigh(where(j), *now)
        kernel_chunk(0, where(j + 2), *now)
        weigh(where(j + 1), *later)
        return carry

    lax.fori_loop(0, main // 2, forward, 0)
    for c in range(own_chunks):
        moment_load(main + c).wait()
    bhi[0, :, span(0)] = now[0][...]
    blo[0, :, span(0)] = now[1][...]
    for c in range(own_chunks):
        if c + 1 < own_chunks:
            kernel_chunk(0, where(main + c + 1), bhi.at[0, :, span(c + 1)], blo.at[0, :, span(c + 1)])
        weigh(where(main + c), *(now if c == 0 else (bhi.at[0, :, span(c)], blo.at[0, :, span(c)])))

    pl.semaphore_wait(barrier, n - 1 + nsub - 1)

    def to_blk(src, dst, ssem, rsem, o, s):
        return pltpu.make_async_remote_copy(
            src_ref=src, dst_ref=dst, send_sem=ssem.at[s], recv_sem=rsem.at[s],
            device_id={"blk": me ^ o}, device_id_type=MESH,
        )

    x_sends = [to_blk(x_ref, xs.at[o - 1], xs_s, xs_r, o, o - 1) for o in range(1, n)]
    for c in x_sends:
        c.start()

    tloads[0].wait()
    lane = lambda h: slice(h * LANES, (h + 1) * LANES)
    for g in range(groups):
        verts = [
            [
                x_ref[d : d + 1, lane(h)] + vel[pl.ds(d * subjects + g * 8, 8), lane(h)]
                for h in range(halves)
            ]
            for d in range(3)
        ]
        ids = [
            [jnp.broadcast_to(tris_ref[k : k + 1, lane(h)], (8, LANES)) for h in range(halves)]
            for k in range(3)
        ]
        for h, (center, one, two, normal) in enumerate(edges(verts, ids)):
            nu = root_norm(normal)
            inv = 1.0 / jnp.sqrt(nu)
            for d in range(3):
                own[d, g, h] = center[d] * SCALE
                own[3 + d, g, h] = normal[d] * inv
                geo[d, g, h] = one[d]
                geo[3 + d, g, h] = two[d]
                geo[6 + d, g, h] = normal[d]
            geo[9, g, h] = nu

    p_sends = [to_blk(own, mates.at[b], pn_s, pn_r, 2**b, b) for b in range(bits)]
    for c in p_sends:
        c.start()

    for c in tloads[1:]:
        c.wait()
    for g in range(groups):
        part = lambda d: pl.ds(d * subjects + g * 8, 8)
        verts = [[tv[part(d), lane(h)] for h in range(halves)] for d in range(3)]
        ids = [[tt[part(k), lane(h)] for h in range(halves)] for k in range(3)]
        for h, (center, one, two, normal) in enumerate(edges(verts, ids)):
            inv = 1.0 / jnp.sqrt(root_norm(normal))
            for d in range(3):
                tgt[d, g, h] = center[d] * SCALE
                tgt[3 + d, g, h] = normal[d] * inv

    for k in range(3):
        vertex = lax.broadcasted_iota(jnp.int32, (elems, elems), 0)
        hot[:, k * elems : (k + 1) * elems] = jnp.where(
            vertex == tris_ref[k : k + 1, :], 1.0, 0.0
        ).astype(bf16)

    every = list(range(halves))
    as_float = lambda v: v.astype(f32)

    def stack(src, q, w, g, h):
        products = [w[d] * q[k] for d in range(3) for k in range(3)]
        for r, value in enumerate(w + products + q + [jnp.zeros_like(q[0])]):
            stk[src, h, pl.ds(g * 8 * ROWS + r, 8, stride=ROWS), :] = value

    for g in range(groups):
        for h in every:
            stack(0, [own[d, g, h] for d in range(3)], [own[3 + d, g, h] for d in range(3)], g, h)
            stack(1, [tgt[d, g, h] for d in range(3)], [tgt[3 + d, g, h] for d in range(3)], g, h)

    wide = lambda parts: jnp.concatenate(parts, axis=1) if len(parts) > 1 else parts[0]
    first = lambda s: s * ROWS if isinstance(s, int) else pl.multiple_of(s * ROWS, ROWS)
    width_of = lambda blocks: slice(0, len(blocks) * LANES)

    def rows_of(s, src, blocks):
        return [stk[src, b, pl.ds(first(s), ROWS), :] for b in blocks]

    def multiply(s, slot, item):
        src, tasks = item
        for own_rows, blocks, _ in tasks:
            hi, lo = split(wide(rows_of(s, src, blocks)))
            inn[slot, own_rows, width_of(blocks)] = mxu(
                uw[s, own_rows, :], jnp.concatenate([hi, lo, hi, lo], axis=0), NN
            )

    def weigh_pairs(s, slot, item):
        src, tasks = item
        for own_rows, blocks, _ in tasks:
            for r in range(own_rows.start, own_rows.stop, 32):
                here = slice(r, r + 32)
                total = None
                for d in range(3):
                    q = wide([stk[src, b, pl.ds(first(s) + 12 + d, 1), :] for b in blocks])
                    off = wide([pb[s, d, here, :]] * len(blocks)) - q
                    total = off * off if total is None else total + off * off
                t = jnp.exp2(-total) * inn[slot, here, width_of(blocks)]
                hi, lo = split(t)
                t_hi[slot, here, width_of(blocks)] = hi
                t_lo[slot, here, width_of(blocks)] = lo

    def collect(s, slot, item, to, fresh):
        src, tasks = item
        for own_rows, blocks, coefs in tasks:
            parts = rows_of(s, src, blocks)
            for a in every:
                if not own_rows.start <= a * LANES < own_rows.stop:
                    continue
                hi, lo = split(wide([part * c for part, c in zip(parts, coefs[a])]))
                both = mxu(
                    jnp.concatenate([hi, lo], axis=0), t_hi[slot, lane(a), width_of(blocks)], NT
                )
                term = both[0:ROWS] + both[ROWS:]
                term = term + mxu(hi, t_lo[slot, lane(a), width_of(blocks)], NT)
                here = pl.ds(first(s), ROWS)
                gout[to, a, here, :] = term if fresh else gout[to, a, here, :] + term

    def sweep(items, to, start, stop, ahead=None):
        last = stop - 1
        many = len(items)
        per = 1 if many % 2 == 0 else 2
        steps = [(ds, x) for ds in range(per) for x in range(many)]

        def body(i, carry):
            s = start + per * i
            before = (jnp.maximum(s - 1, start), many - 1)
            for at_step, (ds, x) in enumerate(steps):
                slot = at_step % 2
                here = s + ds
                collect(before[0], 1 - slot, items[before[1]], to, before[1] == 0)
                weigh_pairs(here, slot, items[x])
                if at_step + 1 < len(steps):
                    more, y = steps[at_step + 1]
                    multiply(s + more, 1 - slot, items[y])
                else:
                    multiply(jnp.minimum(s + per, last), 1 - slot, items[0])
                before = (here, x)
            if ahead is not None:
                for ds in range(per):
                    ahead(jnp.minimum(s + per + 1 + ds, last))
            return carry

        if ahead is not None:
            for s in range(per + 1):
                ahead(start + s)
        multiply(start, 0, items[0])
        lax.fori_loop(0, (stop - start) // per, body, 0)
        collect(last, 1, items[-1], to, many == 1)

    def prepare(s):
        row = lax.broadcasted_iota(jnp.int32, (ROWS, LANES), 0)
        for a in every:
            mine = stk[0, a, pl.ds(first(s), ROWS), :]
            weights = jnp.where(row < 3, mine, 0.0)
            hi = weights.astype(bf16).astype(f32)
            lo = weights - hi
            columns = jnp.concatenate([hi, hi, lo, lo, mine], axis=0).T
            uw[s, lane(a), :] = columns[:, 0 : 4 * ROWS].astype(bf16)
            for d in range(3):
                at_d = 4 * ROWS + 12 + d
                pb[s, d, lane(a), :] = jnp.broadcast_to(columns[:, at_d : at_d + 1], (LANES, LANES))

    whole = slice(0, elems)
    local = {a: [as_float(local_ref[a, b] + local_ref[b, a]) for b in every] for a in every}
    near = [(0, [(whole, every, local)])]
    near.append((1, [(lane(a), [a], {a: [-2.0]}) for a in every]))
    sweep(near, 0, 0, subjects, prepare)

    distant = []
    for bit in range(bits):
        p_sends[bit].wait_recv()
        for g in range(groups):
            for h in every:
                take = lambda d: mates[bit, d, g, h]
                stack(2 + bit, [take(d) for d in range(3)], [take(3 + d) for d in range(3)], g, h)
        coefs = {a: [] for a in every}
        for a in every:
            for b in every:
                count = jnp.int32(0)
                for r in range(4):
                    if r % (n.bit_length() - 1) == bit:
                        count = count + jnp.where(partner_ref[a, r] == b, 2, 0)
                coefs[a].append(as_float(count))
        distant.append((2 + bit, [(whole, every, coefs)]))

    width = 1.0 / LANES
    pack = 3 * 8

    def halve(value):
        hi = value.astype(bf16).astype(f32)
        return jnp.concatenate([hi, value - hi], axis=0).astype(bf16)

    def finish(g):
        corner = [[[None] * halves for _ in range(3)] for _ in range(3)]
        for h in range(halves):
            one = [geo[d, g, h] for d in range(3)]
            two = [geo[3 + d, g, h] for d in range(3)]
            u = [geo[6 + d, g, h] for d in range(3)]
            inv = 1.0 / geo[9, g, h]
            root = jnp.sqrt(geo[9, g, h])
            part = lambda i, r: gout[i, h, pl.ds(g * 8 * ROWS + r, 8, stride=ROWS), :]
            take = lambda r: part(0, r) + part(1, r)
            turned = [root * take(d) for d in range(3)]
            total = u[0] * turned[0] + u[1] * turned[1] + u[2] * turned[2]
            moved = []
            for k in range(3):
                mixed = [u[d] * take(3 + 3 * d + k) for d in range(3)]
                moved.append(own[k, g, h] * total - root * (mixed[0] + mixed[1] + mixed[2]))
            shrink = inv * inv * inv * total
            gp = [moved[d] * inv * (-2.0 * width / SCALE / 3.0) for d in range(3)]
            gu = [(2.0 * inv * turned[d] - u[d] * shrink) * (0.5 * width) for d in range(3)]
            g_one = cross(two, gu)
            g_two = cross(gu, one)
            for d in range(3):
                corner[0][d][h] = gp[d] - g_one[d] - g_two[d]
                corner[1][d][h] = gp[d] + g_one[d]
                corner[2][d][h] = gp[d] + g_two[d]
        value = jnp.concatenate(
            [
                jnp.concatenate([corner[k][d][h] for d in range(3)], axis=0)
                for k in range(3)
                for h in range(halves)
            ],
            axis=1,
        )
        both = mxu(halve(value), hot[...], NT)
        cots[0, g] = both[0:pack] + both[pack:]

    c_sends = []
    for g in range(groups):
        sweep(distant, 1, g * 8, g * 8 + 8)
        finish(g)
        for o in range(1, n):
            at_g = g * (n - 1) + o - 1
            c_sends.append(to_blk(cots.at[0, g], cots.at[o, g], ct_s, ct_r, o, at_g))
            c_sends[-1].start()

    def vel_of(c, g):
        base = c * rows + g * 8
        return jnp.concatenate([vel[pl.ds(base + d * subjects, 8), :] for d in range(3)], axis=0)

    factor = 1.0 / (subjects * nsub)
    over_groups = lambda f: sum(over_rows(f(g, cots[0, g])) for g in range(groups))
    plain = over_groups(lambda g, cot: cot * vel_of(0, g))
    for d in range(3):
        direct = over_groups(lambda g, cot: cot[d * 8 : (d + 1) * 8])
        moved = over_groups(lambda g, cot: cot * vel_of(d + 1, g))
        tgs[sub, pl.ds(d, 1), :] = factor * (direct - 2.0 * (x_ref[d : d + 1, :] * plain - moved))

    g_sends = []
    for o in range(1, nsub):
        g_sends.append(
            pltpu.make_async_remote_copy(
                src_ref=tgs.at[sub], dst_ref=tgs.at[sub], send_sem=tg_s.at[o - 1],
                recv_sem=tg_r.at[o - 1], device_id={"subj": lax.rem(sub + o, nsub)},
                device_id_type=MESH,
            )
        )
    for c in g_sends:
        c.start()

    for o in range(1, n):
        x_sends[o - 1].wait_recv()
        spread(xs[o - 1], o)

    for o in range(1, n):
        for c in range(own_chunks):
            start = pl.multiple_of(me * cdev + c * chunk, chunk)
            kernel_chunk(o, start, bhi.at[o, :, span(c)], blo.at[o, :, span(c)])

    outs = []

    def backward(o):
        halves_of = [cots[o, g] for g in range(groups)]
        value = jnp.concatenate(halves_of, axis=0)
        high = value.astype(bf16).astype(f32)
        two = jnp.concatenate([high, value - high], axis=0).astype(bf16)
        high = high.astype(bf16)

        for c in range(own_chunks):
            both = mxu(two, bhi[o, :, span(c)], NN)
            term = both[0:rows] + both[rows:] + mxu(high, blo[o, :, span(c)], NN)
            for g in range(groups):
                for d in range(3):
                    base = g * pack + d * 8
                    piece = term[base : base + 8]
                    block = pl.ds(d * subjects + g * 8, 8)
                    mg[block, span(c)] = mg[block, span(c)] + piece if o else piece
            if o == n - 1:
                outs.append(
                    pltpu.make_async_copy(mg.at[:, span(c)], mg_hbm.at[:, span(c)], out_sem.at[c])
                )
                outs[-1].start()

    backward(0)
    for o in range(1, n):
        for g in range(groups):
            c_sends[g * (n - 1) + o - 1].wait_recv()
        backward(o)

    for c in g_sends:
        c.wait_recv()
    tg_sum = tgs[0]
    for o in range(1, nsub):
        tg_sum = tg_sum + tgs[o]
    tg_out[...] = tg_sum
    for c in x_sends + p_sends + c_sends + g_sends:
        c.wait_send()
    for c in outs:
        c.wait()


def deliver(tg, mg, tg_out, mg_out, tg_held, held, sem_in, sem_out):
    moves = []
    for d in range(3):
        moves.append(
            (
                pltpu.make_async_copy(mg.at[d], held.at[d], sem_in.at[d]),
                pltpu.make_async_copy(held.at[d], mg_out.at[d], sem_out.at[d]),
            )
        )
    moves.append(
        (
            pltpu.make_async_copy(tg, tg_held, sem_in.at[3]),
            pltpu.make_async_copy(tg_held, tg_out, sem_out.at[3]),
        )
    )
    for c in moves:
        c[0].start()
    for c in moves:
        c[0].wait()
        c[1].start()
    for c in moves:
        c[1].wait()


def on_device(n, nsub, tverts, ttris, local, partner, controls, momenta, tv, tt):
    subjects, _, ctrl = momenta.shape
    elems = tverts.shape[1]
    halves = elems // LANES
    groups = subjects // 8
    rows = 3 * subjects
    cdev = ctrl // n
    bits = min(4, n.bit_length() - 1)
    chunk = min(1024, cdev)
    cfg = (n, nsub, subjects, elems, ctrl, cdev, bits, chunk)
    vmem = pl.BlockSpec(memory_space=pltpu.VMEM)
    hbm = pl.BlockSpec(memory_space=pltpu.HBM)
    panel = (6, groups, halves, 8, LANES)
    dma = pltpu.SemaphoreType.DMA
    by_axis = lambda v: v.transpose(1, 0, 2).reshape(rows, v.shape[2])
    template_grad, grads = pl.pallas_call(
        functools.partial(kernel, cfg),
        out_shape=(
            jax.ShapeDtypeStruct((3, elems), f32),
            jax.ShapeDtypeStruct((rows, cdev), f32),
        ),
        in_specs=[hbm] * 8,
        out_specs=(vmem, hbm),
        scratch_shapes=[
            pltpu.VMEM((3, elems), f32),
            pltpu.VMEM((3, elems), jnp.int32),
            pltpu.SMEM(local.shape, jnp.int32),
            pltpu.SMEM(partner.shape[::-1], jnp.int32),
            pltpu.VMEM((3, ctrl), f32),
            pltpu.VMEM((rows, ctrl), f32),
            pltpu.VMEM((rows, elems), f32),
            pltpu.VMEM((rows, elems), jnp.int32),
            pltpu.VMEM((n - 1, 3, elems), f32),
            pltpu.VMEM((n, elems, 48), bf16),
            pltpu.VMEM((48, ctrl), bf16),
            pltpu.VMEM((elems, chunk), bf16),
            pltpu.VMEM((elems, chunk), bf16),
            pltpu.VMEM((elems, chunk), bf16),
            pltpu.VMEM((elems, chunk), bf16),
            pltpu.VMEM((n, elems, cdev), bf16),
            pltpu.VMEM((n, elems, cdev), bf16),
            pltpu.VMEM((4 * rows, elems), f32),
            pltpu.VMEM(panel, f32),
            pltpu.VMEM(panel, f32),
            pltpu.VMEM((bits,) + panel, f32),
            pltpu.VMEM((2 + bits, halves, subjects * ROWS, LANES), f32),
            pltpu.VMEM((subjects, elems, 4 * ROWS), bf16),
            pltpu.VMEM((subjects, 3, elems, LANES), f32),
            pltpu.VMEM((2, elems, elems), f32),
            pltpu.VMEM((2, elems, elems), bf16),
            pltpu.VMEM((2, elems, elems), bf16),
            pltpu.VMEM((2, halves, subjects * ROWS, LANES), f32),
            pltpu.VMEM((10,) + panel[1:], f32),
            pltpu.VMEM((elems, 3 * elems), bf16),
            pltpu.VMEM((n, groups, 24, elems), f32),
            pltpu.VMEM((rows, cdev), f32),
            pltpu.VMEM((nsub, 3, elems), f32),
            dma((2 + ctrl // chunk,)), dma((5,)),
            dma((n - 1,)), dma((n - 1,)),
            dma((bits,)), dma((bits,)),
            dma((groups * (n - 1),)), dma((groups * (n - 1),)),
            dma((nsub - 1,)), dma((nsub - 1,)),
            dma((cdev // chunk,)),
        ],
        compiler_params=pltpu.CompilerParams(
            collective_id=0, has_side_effects=True, vmem_limit_bytes=64 * 2**20
        ),
        name="atlas",
    )(tverts, ttris, local, partner.T, controls, by_axis(momenta), by_axis(tv), by_axis(tt))
    template_grad, grads = pl.pallas_call(
        deliver,
        out_shape=(
            jax.ShapeDtypeStruct((3, elems), f32),
            jax.ShapeDtypeStruct((3, subjects, cdev), f32),
        ),
        in_specs=[hbm, hbm],
        out_specs=(hbm, hbm),
        scratch_shapes=[
            pltpu.VMEM((3, elems), f32), pltpu.VMEM((3, subjects, cdev), f32), dma((4,)), dma((4,)),
        ],
        name="deliver",
    )(template_grad, grads.reshape(3, subjects, cdev))
    return template_grad, grads.transpose(1, 0, 2)


def solution(mesh):
    return jax.shard_map(
        functools.partial(on_device, mesh.shape["blk"], mesh.shape["subj"]),
        mesh=mesh,
        in_specs=(
            P(None, ("groups", "blk")),
            P(None, ("groups", "blk")),
            P("blk", None),
            P(None, "blk"),
            P(),
            P(("groups", "subj"), None, None),
            P(("groups", "subj"), None, "blk"),
            P(("groups", "subj"), None, "blk"),
        ),
        out_specs=(P(None, ("groups", "blk")), P(("groups", "subj"), None, "blk")),
        check_vma=False,
    )
```

```python
import functools
import math

import jax
import jax.numpy as jnp
from jax import lax
from jax.experimental import pallas as pl
from jax.experimental.pallas import tpu as pltpu
from jax.sharding import PartitionSpec as P

AREA_SQ = 0.25
SCALE = math.sqrt(math.log2(math.e))
LANES = 128
ROWS = 16
MESH = pl.DeviceIdType.MESH
f32, bf16 = jnp.float32, jnp.bfloat16
NT = (((1,), (1,)), ((), ()))
NN = (((1,), (0,)), ((), ()))


def split(value):
    high = value.astype(bf16)
    return high, (value - high.astype(f32)).astype(bf16)


def mxu(a, b, dims):
    return lax.dot_general(a, b, dims, preferred_element_type=f32)


def pick_lanes(halves, indices):
    out = []
    for idx in indices:
        low = idx & (LANES - 1)
        value = jnp.take_along_axis(halves[0], low, axis=1, mode="promise_in_bounds")
        for h in range(1, len(halves)):
            other = jnp.take_along_axis(halves[h], low, axis=1, mode="promise_in_bounds")
            value = jnp.where(idx >= h * LANES, other, value)
        out.append(value)
    return out


def cross(a, b):
    return [
        a[1] * b[2] - a[2] * b[1],
        a[2] * b[0] - a[0] * b[2],
        a[0] * b[1] - a[1] * b[0],
    ]


def edges(verts, corner_ids):
    corners = [[pick_lanes(verts[d], corner_ids[k]) for d in range(3)] for k in range(3)]
    pieces = []
    for h in range(len(corner_ids[0])):
        a, b, c = [[corners[k][d][h] for d in range(3)] for k in range(3)]
        center = [(a[d] + b[d] + c[d]) * (1.0 / 3.0) for d in range(3)]
        one = [b[d] - a[d] for d in range(3)]
        two = [c[d] - a[d] for d in range(3)]
        normal = [0.5 * v for v in cross(one, two)]
        pieces.append((center, one, two, normal))
    return pieces


def root_norm(normal):
    return jnp.sqrt(normal[0] * normal[0] + normal[1] * normal[1] + normal[2] * normal[2] + AREA_SQ)


def kernel(
    cfg,
    x_hbm, tris_hbm, local_hbm, partner_hbm, ctrl_hbm, mom_hbm, tv_hbm, tt_hbm,
    tg_out, mg_hbm,
    x_ref, tris_ref, local_ref, partner_ref, ctrl_ref, mom, tv, tt, xs, xl, csc, khi, klo, khi_b, klo_b, bhi, blo, vel, own, tgt, mates, stk, uw, pb, inn, t_hi, t_lo, gout, geo, hot, cots, mg, tgs,
    mom_sem, t_sem, xs_s, xs_r, pn_s, pn_r, ct_s, ct_r, tg_s, tg_r, out_sem,
):
    n, nsub, subjects, elems, ctrl, cdev, bits, chunk = cfg
    rows = 3 * subjects
    halves = elems // LANES
    groups = subjects // 8
    me = lax.axis_index("blk")
    sub = lax.axis_index("subj")

    loads = [
        pltpu.make_async_copy(x_hbm, x_ref, mom_sem.at[0]),
        pltpu.make_async_copy(ctrl_hbm, ctrl_ref, mom_sem.at[1]),
    ]
    tloads = [
        pltpu.make_async_copy(tris_hbm, tris_ref, t_sem.at[0]),
        pltpu.make_async_copy(tv_hbm, tv, t_sem.at[1]),
        pltpu.make_async_copy(tt_hbm, tt, t_sem.at[2]),
        pltpu.make_async_copy(local_hbm, local_ref, t_sem.at[3]),
        pltpu.make_async_copy(partner_hbm, partner_ref, t_sem.at[4]),
    ]
    def moment_load(j):
        here = pl.ds(pl.multiple_of(lax.rem((me + 1) * cdev + j * chunk, ctrl), chunk), chunk)
        return pltpu.make_async_copy(mom_hbm.at[:, here], mom.at[:, here], mom_sem.at[2 + j])

    for c in loads:
        c.start()
    for j in range(ctrl // chunk):
        moment_load(j).start()
    for c in tloads:
        c.start()

    def over_rows(value):
        return jnp.sum(value, axis=0, keepdims=True)

    barrier = pltpu.get_barrier_semaphore()
    for o in range(1, n):
        pl.semaphore_signal(barrier, inc=1, device_id={"blk": me ^ o}, device_id_type=MESH)
    for o in range(1, nsub):
        pl.semaphore_signal(
            barrier, inc=1, device_id={"subj": lax.rem(sub + o, nsub)}, device_id_type=MESH
        )

    def augment(points, near, factor):
        scaled = points * SCALE
        square = over_rows(scaled * scaled)
        ones = jnp.full_like(square, near)
        pair = [ones, square * near] if near < 0 else [square, ones]
        rest = jnp.zeros((3, points.shape[1]), f32)
        return jnp.concatenate([scaled * factor] + pair + [rest], axis=0)

    def thirds(value):
        one = value.astype(bf16).astype(f32)
        two = (value - one).astype(bf16).astype(f32)
        return one, two, value - one - two

    def spread(points, slot):
        b1, b2, b3 = thirds(augment(points, -1.0, 2.0))
        xl[slot] = jnp.concatenate([b1, b1, b2, b2, b1, b3], axis=0).T.astype(bf16)

    loads[0].wait()
    spread(x_ref[...], 0)
    loads[1].wait()
    for i in range(0, ctrl, 1024):
        here = slice(i, i + 1024)
        a1, a2, a3 = thirds(augment(ctrl_ref[:, here], 1.0, 1.0))
        csc[:, here] = jnp.concatenate([a1, a2, a1, a2, a3, a1], axis=0).astype(bf16)
    vel[...] = jnp.zeros_like(vel)

    def kernel_chunk(slot, start, hi_to, lo_to):
        power = mxu(xl[slot], csc[:, pl.ds(start, chunk)], NN)
        hi, lo = split(jnp.exp2(power))
        hi_to[...] = hi
        lo_to[...] = lo


    def weigh(start, hi_from, lo_from):
        m = mom[:, pl.ds(start, chunk)]
        weighted = [m]
        for d in range(3):
            weighted.append(m * ctrl_ref[d : d + 1, pl.ds(start, chunk)])
        pairs = [split(w) for w in weighted]
        hi = jnp.concatenate([p[0] for p in pairs], axis=0)
        both = mxu(jnp.concatenate([hi] + [p[1] for p in pairs], axis=0), hi_from[...], NT)
        vel[...] += both[0 : 4 * rows] + both[4 * rows :] + mxu(hi, lo_from[...], NT)

    own_chunks = cdev // chunk
    main = ctrl // chunk - own_chunks
    span = lambda c: slice(c * chunk, (c + 1) * chunk)

    def where(j):
        return pl.multiple_of(lax.rem((me + 1) * cdev + j * chunk, ctrl), chunk)

    now, later = (khi, klo), (khi_b, klo_b)
    kernel_chunk(0, where(0), *now)
    odd = main % 2
    if odd:
        moment_load(0).wait()
        kernel_chunk(0, where(1), *later)
        weigh(where(0), *now)
        now, later = later, now

    def forward(i, carry):
        j = odd + 2 * i
        moment_load(j).wait()
        moment_load(j + 1).wait()
        kernel_chunk(0, where(j + 1), *later)
        weigh(where(j), *now)
        kernel_chunk(0, where(j + 2), *now)
        weigh(where(j + 1), *later)
        return carry

    lax.fori_loop(0, main // 2, forward, 0)
    for c in range(own_chunks):
        moment_load(main + c).wait()
    bhi[0, :, span(0)] = now[0][...]
    blo[0, :, span(0)] = now[1][...]
    for c in range(own_chunks):
        if c + 1 < own_chunks:
            kernel_chunk(0, where(main + c + 1), bhi.at[0, :, span(c + 1)], blo.at[0, :, span(c + 1)])
        weigh(where(main + c), *(now if c == 0 else (bhi.at[0, :, span(c)], blo.at[0, :, span(c)])))

    pl.semaphore_wait(barrier, n - 1 + nsub - 1)

    def to_blk(src, dst, ssem, rsem, o, s):
        return pltpu.make_async_remote_copy(
            src_ref=src, dst_ref=dst, send_sem=ssem.at[s], recv_sem=rsem.at[s],
            device_id={"blk": me ^ o}, device_id_type=MESH,
        )

    x_sends = [to_blk(x_ref, xs.at[o - 1], xs_s, xs_r, o, o - 1) for o in range(1, n)]
    for c in x_sends:
        c.start()

    tloads[0].wait()
    lane = lambda h: slice(h * LANES, (h + 1) * LANES)
    for g in range(groups):
        verts = [
            [
                x_ref[d : d + 1, lane(h)] + vel[pl.ds(d * subjects + g * 8, 8), lane(h)]
                for h in range(halves)
            ]
            for d in range(3)
        ]
        ids = [
            [jnp.broadcast_to(tris_ref[k : k + 1, lane(h)], (8, LANES)) for h in range(halves)]
            for k in range(3)
        ]
        for h, (center, one, two, normal) in enumerate(edges(verts, ids)):
            nu = root_norm(normal)
            inv = 1.0 / jnp.sqrt(nu)
            for d in range(3):
                own[d, g, h] = center[d] * SCALE
                own[3 + d, g, h] = normal[d] * inv
                geo[d, g, h] = one[d]
                geo[3 + d, g, h] = two[d]
                geo[6 + d, g, h] = normal[d]
            geo[9, g, h] = nu

    p_sends = [to_blk(own, mates.at[b], pn_s, pn_r, 2**b, b) for b in range(bits)]
    for c in p_sends:
        c.start()

    for c in tloads[1:]:
        c.wait()
    for g in range(groups):
        part = lambda d: pl.ds(d * subjects + g * 8, 8)
        verts = [[tv[part(d), lane(h)] for h in range(halves)] for d in range(3)]
        ids = [[tt[part(k), lane(h)] for h in range(halves)] for k in range(3)]
        for h, (center, one, two, normal) in enumerate(edges(verts, ids)):
            inv = 1.0 / jnp.sqrt(root_norm(normal))
            for d in range(3):
                tgt[d, g, h] = center[d] * SCALE
                tgt[3 + d, g, h] = normal[d] * inv

    for k in range(3):
        vertex = lax.broadcasted_iota(jnp.int32, (elems, elems), 0)
        hot[:, k * elems : (k + 1) * elems] = jnp.where(
            vertex == tris_ref[k : k + 1, :], 1.0, 0.0
        ).astype(bf16)

    every = list(range(halves))
    as_float = lambda v: v.astype(f32)

    def stack(src, q, w, g, h):
        products = [w[d] * q[k] for d in range(3) for k in range(3)]
        for r, value in enumerate(w + products + q + [jnp.zeros_like(q[0])]):
            stk[src, h, pl.ds(g * 8 * ROWS + r, 8, stride=ROWS), :] = value

    for g in range(groups):
        for h in every:
            stack(0, [own[d, g, h] for d in range(3)], [own[3 + d, g, h] for d in range(3)], g, h)
            stack(1, [tgt[d, g, h] for d in range(3)], [tgt[3 + d, g, h] for d in range(3)], g, h)

    wide = lambda parts: jnp.concatenate(parts, axis=1) if len(parts) > 1 else parts[0]
    first = lambda s: s * ROWS if isinstance(s, int) else pl.multiple_of(s * ROWS, ROWS)
    width_of = lambda blocks: slice(0, len(blocks) * LANES)

    def rows_of(s, src, blocks):
        return [stk[src, b, pl.ds(first(s), ROWS), :] for b in blocks]

    def multiply(s, slot, item):
        src, tasks = item
        for own_rows, blocks, _ in tasks:
            hi, lo = split(wide(rows_of(s, src, blocks)))
            inn[slot, own_rows, width_of(blocks)] = mxu(
                uw[s, own_rows, :], jnp.concatenate([hi, lo, hi, lo], axis=0), NN
            )

    def weigh_pairs(s, slot, item):
        src, tasks = item
        for own_rows, blocks, _ in tasks:
            for r in range(own_rows.start, own_rows.stop, 16):
                here = slice(r, r + 16)
                total = None
                for d in range(3):
                    q = wide([stk[src, b, pl.ds(first(s) + 12 + d, 1), :] for b in blocks])
                    off = wide([pb[s, d, here, :]] * len(blocks)) - q
                    total = off * off if total is None else total + off * off
                t = jnp.exp2(-total) * inn[slot, here, width_of(blocks)]
                hi, lo = split(t)
                t_hi[slot, here, width_of(blocks)] = hi
                t_lo[slot, here, width_of(blocks)] = lo

    def collect(s, slot, item, to, fresh):
        src, tasks = item
        for own_rows, blocks, coefs in tasks:
            parts = rows_of(s, src, blocks)
            for a in every:
                if not own_rows.start <= a * LANES < own_rows.stop:
                    continue
                hi, lo = split(wide([part * c for part, c in zip(parts, coefs[a])]))
                both = mxu(
                    jnp.concatenate([hi, lo], axis=0), t_hi[slot, lane(a), width_of(blocks)], NT
                )
                term = both[0:ROWS] + both[ROWS:]
                term = term + mxu(hi, t_lo[slot, lane(a), width_of(blocks)], NT)
                here = pl.ds(first(s), ROWS)
                gout[to, a, here, :] = term if fresh else gout[to, a, here, :] + term

    def sweep(items, to, start, stop, ahead=None):
        last = stop - 1
        many = len(items)
        per = 1 if many % 2 == 0 else 2
        steps = [(ds, x) for ds in range(per) for x in range(many)]

        def body(i, carry):
            s = start + per * i
            before = (jnp.maximum(s - 1, start), many - 1)
            for at_step, (ds, x) in enumerate(steps):
                slot = at_step % 2
                here = s + ds
                collect(before[0], 1 - slot, items[before[1]], to, before[1] == 0)
                weigh_pairs(here, slot, items[x])
                if at_step + 1 < len(steps):
                    more, y = steps[at_step + 1]
                    multiply(s + more, 1 - slot, items[y])
                else:
                    multiply(jnp.minimum(s + per, last), 1 - slot, items[0])
                before = (here, x)
            if ahead is not None:
                for ds in range(per):
                    ahead(jnp.minimum(s + per + 1 + ds, last))
            return carry

        if ahead is not None:
            for s in range(per + 1):
                ahead(start + s)
        multiply(start, 0, items[0])
        lax.fori_loop(0, (stop - start) // per, body, 0)
        collect(last, 1, items[-1], to, many == 1)

    def prepare(s):
        row = lax.broadcasted_iota(jnp.int32, (ROWS, LANES), 0)
        for a in every:
            mine = stk[0, a, pl.ds(first(s), ROWS), :]
            weights = jnp.where(row < 3, mine, 0.0)
            hi = weights.astype(bf16).astype(f32)
            lo = weights - hi
            columns = jnp.concatenate([hi, hi, lo, lo, mine], axis=0).T
            uw[s, lane(a), :] = columns[:, 0 : 4 * ROWS].astype(bf16)
            for d in range(3):
                at_d = 4 * ROWS + 12 + d
                pb[s, d, lane(a), :] = jnp.broadcast_to(columns[:, at_d : at_d + 1], (LANES, LANES))

    whole = slice(0, elems)
    local = {a: [as_float(local_ref[a, b] + local_ref[b, a]) for b in every] for a in every}
    near = [(0, [(whole, every, local)])]
    near.append((1, [(lane(a), [a], {a: [-2.0]}) for a in every]))
    sweep(near, 0, 0, subjects, prepare)

    distant = []
    for bit in range(bits):
        p_sends[bit].wait_recv()
        for g in range(groups):
            for h in every:
                take = lambda d: mates[bit, d, g, h]
                stack(2 + bit, [take(d) for d in range(3)], [take(3 + d) for d in range(3)], g, h)
        coefs = {a: [] for a in every}
        for a in every:
            for b in every:
                count = jnp.int32(0)
                for r in range(4):
                    if r % (n.bit_length() - 1) == bit:
                        count = count + jnp.where(partner_ref[a, r] == b, 2, 0)
                coefs[a].append(as_float(count))
        distant.append((2 + bit, [(whole, every, coefs)]))

    width = 1.0 / LANES
    pack = 3 * 8

    def halve(value):
        hi = value.astype(bf16).astype(f32)
        return jnp.concatenate([hi, value - hi], axis=0).astype(bf16)

    def finish(g):
        corner = [[[None] * halves for _ in range(3)] for _ in range(3)]
        for h in range(halves):
            one = [geo[d, g, h] for d in range(3)]
            two = [geo[3 + d, g, h] for d in range(3)]
            u = [geo[6 + d, g, h] for d in range(3)]
            inv = 1.0 / geo[9, g, h]
            root = jnp.sqrt(geo[9, g, h])
            part = lambda i, r: gout[i, h, pl.ds(g * 8 * ROWS + r, 8, stride=ROWS), :]
            take = lambda r: part(0, r) + part(1, r)
            turned = [root * take(d) for d in range(3)]
            total = u[0] * turned[0] + u[1] * turned[1] + u[2] * turned[2]
            moved = []
            for k in range(3):
                mixed = [u[d] * take(3 + 3 * d + k) for d in range(3)]
                moved.append(own[k, g, h] * total - root * (mixed[0] + mixed[1] + mixed[2]))
            shrink = inv * inv * inv * total
            gp = [moved[d] * inv * (-2.0 * width / SCALE / 3.0) for d in range(3)]
            gu = [(2.0 * inv * turned[d] - u[d] * shrink) * (0.5 * width) for d in range(3)]
            g_one = cross(two, gu)
            g_two = cross(gu, one)
            for d in range(3):
                corner[0][d][h] = gp[d] - g_one[d] - g_two[d]
                corner[1][d][h] = gp[d] + g_one[d]
                corner[2][d][h] = gp[d] + g_two[d]
        value = jnp.concatenate(
            [
                jnp.concatenate([corner[k][d][h] for d in range(3)], axis=0)
                for k in range(3)
                for h in range(halves)
            ],
            axis=1,
        )
        both = mxu(halve(value), hot[...], NT)
        cots[0, g] = both[0:pack] + both[pack:]

    c_sends = []
    for g in range(groups):
        sweep(distant, 1, g * 8, g * 8 + 8)
        finish(g)
        for o in range(1, n):
            at_g = g * (n - 1) + o - 1
            c_sends.append(to_blk(cots.at[0, g], cots.at[o, g], ct_s, ct_r, o, at_g))
            c_sends[-1].start()

    def vel_of(c, g):
        base = c * rows + g * 8
        return jnp.concatenate([vel[pl.ds(base + d * subjects, 8), :] for d in range(3)], axis=0)

    factor = 1.0 / (subjects * nsub)
    over_groups = lambda f: sum(over_rows(f(g, cots[0, g])) for g in range(groups))
    plain = over_groups(lambda g, cot: cot * vel_of(0, g))
    for d in range(3):
        direct = over_groups(lambda g, cot: cot[d * 8 : (d + 1) * 8])
        moved = over_groups(lambda g, cot: cot * vel_of(d + 1, g))
        tgs[sub, pl.ds(d, 1), :] = factor * (direct - 2.0 * (x_ref[d : d + 1, :] * plain - moved))

    g_sends = []
    for o in range(1, nsub):
        g_sends.append(
            pltpu.make_async_remote_copy(
                src_ref=tgs.at[sub], dst_ref=tgs.at[sub], send_sem=tg_s.at[o - 1],
                recv_sem=tg_r.at[o - 1], device_id={"subj": lax.rem(sub + o, nsub)},
                device_id_type=MESH,
            )
        )
    for c in g_sends:
        c.start()

    for o in range(1, n):
        x_sends[o - 1].wait_recv()
        spread(xs[o - 1], o)

    for o in range(1, n):
        for c in range(own_chunks):
            start = pl.multiple_of(me * cdev + c * chunk, chunk)
            kernel_chunk(o, start, bhi.at[o, :, span(c)], blo.at[o, :, span(c)])

    outs = []

    def backward(o):
        halves_of = [cots[o, g] for g in range(groups)]
        value = jnp.concatenate(halves_of, axis=0)
        high = value.astype(bf16).astype(f32)
        two = jnp.concatenate([high, value - high], axis=0).astype(bf16)
        high = high.astype(bf16)

        for c in range(own_chunks):
            both = mxu(two, bhi[o, :, span(c)], NN)
            term = both[0:rows] + both[rows:] + mxu(high, blo[o, :, span(c)], NN)
            for g in range(groups):
                for d in range(3):
                    base = g * pack + d * 8
                    piece = term[base : base + 8]
                    block = pl.ds(d * subjects + g * 8, 8)
                    mg[block, span(c)] = mg[block, span(c)] + piece if o else piece
            if o == n - 1:
                outs.append(
                    pltpu.make_async_copy(mg.at[:, span(c)], mg_hbm.at[:, span(c)], out_sem.at[c])
                )
                outs[-1].start()

    backward(0)
    for o in range(1, n):
        for g in range(groups):
            c_sends[g * (n - 1) + o - 1].wait_recv()
        backward(o)

    for c in g_sends:
        c.wait_recv()
    tg_sum = tgs[0]
    for o in range(1, nsub):
        tg_sum = tg_sum + tgs[o]
    tg_out[...] = tg_sum
    for c in x_sends + p_sends + c_sends + g_sends:
        c.wait_send()
    for c in outs:
        c.wait()


def deliver(tg, mg, tg_out, mg_out, tg_held, held, sem_in, sem_out):
    moves = []
    for d in range(3):
        moves.append(
            (
                pltpu.make_async_copy(mg.at[d], held.at[d], sem_in.at[d]),
                pltpu.make_async_copy(held.at[d], mg_out.at[d], sem_out.at[d]),
            )
        )
    moves.append(
        (
            pltpu.make_async_copy(tg, tg_held, sem_in.at[3]),
            pltpu.make_async_copy(tg_held, tg_out, sem_out.at[3]),
        )
    )
    for c in moves:
        c[0].start()
    for c in moves:
        c[0].wait()
        c[1].start()
    for c in moves:
        c[1].wait()


def on_device(n, nsub, tverts, ttris, local, partner, controls, momenta, tv, tt):
    subjects, _, ctrl = momenta.shape
    elems = tverts.shape[1]
    halves = elems // LANES
    groups = subjects // 8
    rows = 3 * subjects
    cdev = ctrl // n
    bits = min(4, n.bit_length() - 1)
    chunk = min(1024, cdev)
    cfg = (n, nsub, subjects, elems, ctrl, cdev, bits, chunk)
    vmem = pl.BlockSpec(memory_space=pltpu.VMEM)
    hbm = pl.BlockSpec(memory_space=pltpu.HBM)
    panel = (6, groups, halves, 8, LANES)
    dma = pltpu.SemaphoreType.DMA
    by_axis = lambda v: v.transpose(1, 0, 2).reshape(rows, v.shape[2])
    template_grad, grads = pl.pallas_call(
        functools.partial(kernel, cfg),
        out_shape=(
            jax.ShapeDtypeStruct((3, elems), f32),
            jax.ShapeDtypeStruct((rows, cdev), f32),
        ),
        in_specs=[hbm] * 8,
        out_specs=(vmem, hbm),
        scratch_shapes=[
            pltpu.VMEM((3, elems), f32),
            pltpu.VMEM((3, elems), jnp.int32),
            pltpu.SMEM(local.shape, jnp.int32),
            pltpu.SMEM(partner.shape[::-1], jnp.int32),
            pltpu.VMEM((3, ctrl), f32),
            pltpu.VMEM((rows, ctrl), f32),
            pltpu.VMEM((rows, elems), f32),
            pltpu.VMEM((rows, elems), jnp.int32),
            pltpu.VMEM((n - 1, 3, elems), f32),
            pltpu.VMEM((n, elems, 48), bf16),
            pltpu.VMEM((48, ctrl), bf16),
            pltpu.VMEM((elems, chunk), bf16),
            pltpu.VMEM((elems, chunk), bf16),
            pltpu.VMEM((elems, chunk), bf16),
            pltpu.VMEM((elems, chunk), bf16),
            pltpu.VMEM((n, elems, cdev), bf16),
            pltpu.VMEM((n, elems, cdev), bf16),
            pltpu.VMEM((4 * rows, elems), f32),
            pltpu.VMEM(panel, f32),
            pltpu.VMEM(panel, f32),
            pltpu.VMEM((bits,) + panel, f32),
            pltpu.VMEM((2 + bits, halves, subjects * ROWS, LANES), f32),
            pltpu.VMEM((subjects, elems, 4 * ROWS), bf16),
            pltpu.VMEM((subjects, 3, elems, LANES), f32),
            pltpu.VMEM((2, elems, elems), f32),
            pltpu.VMEM((2, elems, elems), bf16),
            pltpu.VMEM((2, elems, elems), bf16),
            pltpu.VMEM((2, halves, subjects * ROWS, LANES), f32),
            pltpu.VMEM((10,) + panel[1:], f32),
            pltpu.VMEM((elems, 3 * elems), bf16),
            pltpu.VMEM((n, groups, 24, elems), f32),
            pltpu.VMEM((rows, cdev), f32),
            pltpu.VMEM((nsub, 3, elems), f32),
            dma((2 + ctrl // chunk,)), dma((5,)),
            dma((n - 1,)), dma((n - 1,)),
            dma((bits,)), dma((bits,)),
            dma((groups * (n - 1),)), dma((groups * (n - 1),)),
            dma((nsub - 1,)), dma((nsub - 1,)),
            dma((cdev // chunk,)),
        ],
        compiler_params=pltpu.CompilerParams(
            collective_id=0, has_side_effects=True, vmem_limit_bytes=64 * 2**20
        ),
        name="atlas",
    )(tverts, ttris, local, partner.T, controls, by_axis(momenta), by_axis(tv), by_axis(tt))
    template_grad, grads = pl.pallas_call(
        deliver,
        out_shape=(
            jax.ShapeDtypeStruct((3, elems), f32),
            jax.ShapeDtypeStruct((3, subjects, cdev), f32),
        ),
        in_specs=[hbm, hbm],
        out_specs=(hbm, hbm),
        scratch_shapes=[
            pltpu.VMEM((3, elems), f32), pltpu.VMEM((3, subjects, cdev), f32), dma((4,)), dma((4,)),
        ],
        name="deliver",
    )(template_grad, grads.reshape(3, subjects, cdev))
    return template_grad, grads.transpose(1, 0, 2)


def solution(mesh):
    return jax.shard_map(
        functools.partial(on_device, mesh.shape["blk"], mesh.shape["subj"]),
        mesh=mesh,
        in_specs=(
            P(None, ("groups", "blk")),
            P(None, ("groups", "blk")),
            P("blk", None),
            P(None, "blk"),
            P(),
            P(("groups", "subj"), None, None),
            P(("groups", "subj"), None, "blk"),
            P(("groups", "subj"), None, "blk"),
        ),
        out_specs=(P(None, ("groups", "blk")), P(("groups", "subj"), None, "blk")),
        check_vma=False,
    )
```
